32 devices in a mesh: tm: 16 (over z, y, core), video: 2 (over x).
Axes of the slice: x: 2, y: 2, z: 4, core: 2. Of those that a mesh axis runs over, the one named last changes fastest.
Arguments:
- memory: bfloat16 [2, 16, 1, 64, 768], P('video', 'tm'), may hold values from -24 to 24
- frames: float32 [2, 16, 1, 128, 768], P('video', 'tm'), may hold values from -6 to 6
- mem_cot: bfloat16 [2, 16, 1, 64, 768], P('video', 'tm'), may hold values from -3 to 3
- slot_used: int32 [2, 16, 1], P('video', 'tm'), may hold values 0 or 1
- key_bias: float32 [2, 16, 1, 12, 128], P('video', 'tm'), may hold values from -6 to 300
- start_offset: int32 [2, 1], P('video'), may hold values from 0 to 2047
- norm_gain: float32 [768], replicated, may hold values from 0.5 to 1.5
- w_query: bfloat16 [768, 768], replicated, may hold values from -0.21875 to 0.21875
- w_key: bfloat16 [768, 768], replicated, may hold values from -0.21875 to 0.21875
- w_value: bfloat16 [768, 768], replicated, may hold values from -0.21875 to 0.21875
- w_out: bfloat16 [768, 768], replicated, may hold values from -0.21875 to 0.21875
Outputs:
- grad_memory: float32 [2, 16, 1, 64, 768], P('video', 'tm')
- grad_query: float32 [768, 768], P('tm', 'video')
- grad_key: float32 [768, 768], P('tm', 'video')
- grad_value: float32 [768, 768], P('tm', 'video')
- grad_out: float32 [768, 768], P('tm', 'video')
- grad_gain: float32 [768], replicated
The draws below stay inside these ranges and needn't reach their ends.
All inputs are finite; a program needn't handle non-finite values. No bound on the sum of `slot_used` on one device may be relied on, other than what follows from the above.
Results may differ from the reference program's by a relative error of at most 0.019.
Values sent between devices are 32-bit elements; how exact they have to be, the bound alone decides.
A program may use at most 64 MiB of HBM per device.

```python
import math
import jax
import jax.numpy as jnp
from jax import lax

D = 768
H = 12
HD = 64
R = 64
L = 128
STREAMS = 1
GROUPS = 2
OWNERS = 16


def draw_memory(key, part):
    full_shape = (GROUPS, OWNERS, STREAMS, R, D)
    key_noise, key_rows, key_cols = jax.random.split(key, 3)
    gaussian = jax.random.normal(key_noise, full_shape, jnp.float32)
    row_scale = jnp.exp(jax.random.uniform(key_rows, full_shape[:4] + (1,), jnp.float32, math.log(0.3), math.log(3.0)))
    column_scale = jnp.exp(jax.random.uniform(key_cols, (D,), jnp.float32, math.log(0.3), math.log(3.0)))
    values_drawn = gaussian * row_scale * column_scale
    return jnp.clip(values_drawn, -24.0, 24.0).astype(jnp.bfloat16)


def draw_key_bias(key, part):
    full_shape = (GROUPS, OWNERS, STREAMS, H, L)
    key_noise = jax.random.fold_in(key, 0)
    values_drawn = jnp.clip(jax.random.normal(key_noise, full_shape, jnp.float32), -6.0, 6.0)
    return values_drawn


def with_ends(entries, stream_key, least, top_value):
    shape = entries.shape
    index_at = [jax.random.randint(jax.random.fold_in(stream_key, axis), (), 0, shape[axis]) for axis in range(len(shape))]
    entries = entries.at[tuple(index_at)].set(least)
    longest = shape.index(max(shape))
    index_at[longest] = (index_at[longest] + 1) % shape[longest]
    return entries.at[tuple(index_at)].set(top_value)


def block_levels(stream_key, shape, cuts, low, high):
    def one(dim, blocks):
        heights = jax.random.uniform(jax.random.fold_in(jax.random.fold_in(stream_key, 6), dim), (blocks,), jnp.float32, low / len(cuts), high / len(cuts))
        return jnp.repeat(jnp.exp(heights), shape[dim] // blocks).reshape((-1,) + (1,) * (len(shape) - dim - 1))

    loudness = one(*cuts[0])
    for cut in cuts[1:]:
        loudness = loudness * one(*cut)
    return loudness


def normal_values(key, dims, scale, bound, cuts=(), kind=jnp.bfloat16):
    result = jax.random.normal(key, dims, jnp.float32) * scale
    if len(cuts) > 0:
        result = block_levels(key, dims, cuts, -0.22, 0.18) * result
    return jnp.clip(result, min=-bound, max=bound).astype(kind)


def setup_inputs(seed: int = 0) -> dict:
    key_list = jax.random.split(jax.random.key(seed), 12)
    return {
        "memory": draw_memory(jax.random.fold_in(key_list[11], 71), 0),
        "frames": normal_values(key_list[1], (GROUPS, OWNERS, STREAMS, L, D), 1.0, 6.0, ((0, 2), (1, 16)), jnp.float32),
        "mem_cot": normal_values(key_list[2], (GROUPS, OWNERS, STREAMS, R, D), 0.5, 3.0, ((0, 2), (1, 16))),
        "slot_used": with_ends((jax.random.randint(key_list[3], (GROUPS, OWNERS, STREAMS), 0, 4) < 3).astype(jnp.int32), jax.random.fold_in(key_list[3], 1), 0, 1),
        "key_bias": draw_key_bias(jax.random.fold_in(key_list[11], 71), 0),
        "start_offset": jax.random.randint(key_list[5], (GROUPS, STREAMS), 0, L * OWNERS).astype(jnp.int32),
        "norm_gain": jnp.clip(1.0 + 0.1 * jax.random.normal(key_list[6], (D,), jnp.float32), 0.5, 1.5),
        "w_query": normal_values(key_list[7], (D, D), D ** -0.5, 0.21875),
        "w_key": normal_values(key_list[8], (D, D), D ** -0.5, 0.21875),
        "w_value": normal_values(key_list[9], (D, D), D ** -0.5, 0.21875),
        "w_out": normal_values(key_list[10], (D, D), D ** -0.5, 0.21875),
    }


NORM_EPSILON = 1e-06

def product(form, left, right):
    return jnp.einsum(form, left.astype(jnp.float32), right.astype(jnp.float32), precision=lax.Precision.HIGHEST)

def encoding(offsets, position, clip_len, features):
    within = jnp.arange(clip_len, dtype=jnp.int32)
    frame_time = offsets[:, None] + position * clip_len + within[None, :]
    half_width = features // 2
    frequency = 0.0625 * jnp.exp(-math.log(1000.0) * jnp.arange(half_width, dtype=jnp.float32) / half_width)
    phases = frame_time.astype(jnp.float32)[:, :, None] * frequency
    return jnp.concatenate([jnp.sin(phases), jnp.cos(phases)], axis=-1)

def recompute(memory_full, frame_rows, bias_rows, offsets, position, norm_gain, w_query, w_key, w_value):
    batch, row_count, features = memory_full.shape
    inv_rms = lax.rsqrt(lax.optimization_barrier(jnp.mean(memory_full * memory_full, axis=-1, keepdims=True)) + NORM_EPSILON)
    unit_rows = memory_full * inv_rms
    normed = (unit_rows * norm_gain).astype(jnp.bfloat16)
    key_input = (frame_rows + encoding(offsets, position, frame_rows.shape[1], features)).astype(jnp.bfloat16)
    query_proj = product('brd,de->bre', normed, w_query).astype(jnp.bfloat16)
    key_proj = product('bld,de->ble', key_input, w_key).astype(jnp.bfloat16)
    value_proj = product('bld,de->ble', key_input, w_value).astype(jnp.bfloat16)
    query_heads = query_proj.reshape(batch, row_count, H, HD)
    key_heads = key_proj.reshape(batch, -1, H, HD)
    value_heads = value_proj.reshape(batch, -1, H, HD)
    scores = product('brhd,blhd->bhrl', query_heads, key_heads) * HD ** (-0.5) + bias_rows[:, :, None, :]
    attn_prob = jax.nn.softmax(scores, axis=-1)
    attn_half = attn_prob.astype(jnp.bfloat16)
    attended = product('bhrl,blhd->brhd', attn_half, value_heads).astype(jnp.bfloat16).reshape(batch, row_count, features)
    return (inv_rms, unit_rows, normed, key_input, query_heads, key_heads, value_heads, attn_prob, attn_half, attended)

def chain_part(grad_in, slot_live, unit_rows, inv_rms, attn_prob, key_heads, value_heads, norm_gain, w_query, w_out):
    batch, row_count, features = grad_in.shape
    out_grad = (slot_live[:, None, None] * grad_in).astype(jnp.bfloat16)
    att_grad = product('bre,de->brd', out_grad, w_out).astype(jnp.bfloat16)
    att_heads = att_grad.reshape(batch, row_count, H, HD)
    prob_grad = product('brhd,blhd->bhrl', att_heads, value_heads)
    inner_sum = lax.optimization_barrier(jnp.sum(attn_prob * prob_grad, axis=-1, keepdims=True))
    score_grad = (attn_prob * (prob_grad - inner_sum) * HD ** (-0.5)).astype(jnp.bfloat16)
    query_grad = product('bhrl,blhd->brhd', score_grad, key_heads).astype(jnp.bfloat16).reshape(batch, row_count, features)
    normed_grad = product('bre,de->brd', query_grad, w_query)
    gain_term = lax.optimization_barrier(jnp.sum(normed_grad * unit_rows, axis=(0, 1)))
    scaled_grad = normed_grad * norm_gain
    passed = grad_in + inv_rms * (scaled_grad - unit_rows * lax.optimization_barrier(jnp.mean(scaled_grad * unit_rows, axis=-1, keepdims=True)))
    return (passed, out_grad, att_heads, score_grad, query_grad, gain_term)

def weight_part(normed, key_input, query_heads, attn_half, attended, out_grad, att_heads, score_grad, query_grad):
    batch, length, features = key_input.shape
    value_grad = product('bhrl,brhd->blhd', attn_half, att_heads).astype(jnp.bfloat16).reshape(batch, length, features)
    key_grad = product('bhrl,brhd->blhd', score_grad, query_heads).astype(jnp.bfloat16).reshape(batch, length, features)
    return (product('brd,bre->de', normed, query_grad), product('bld,ble->de', key_input, key_grad), product('bld,ble->de', key_input, value_grad), product('brd,bre->de', attended, out_grad))

def reference(memory, frames, mem_cot, slot_used, key_bias, start_offset, norm_gain, w_query, w_key, w_value, w_out):
    groups, owners, streams, row_count, features = memory.shape
    batch = groups * streams
    offsets = start_offset.reshape(batch)

    def take(array, owner):
        picked = lax.dynamic_index_in_dim(array, owner, 1, keepdims=False)
        return picked.reshape((batch,) + picked.shape[2:])

    def one_clip(carried, owner):
        incoming, sum_query, sum_key, sum_value, sum_out, sum_gain = carried
        parts = recompute(take(memory, owner).astype(jnp.float32), take(frames, owner), take(key_bias, owner), offsets, owner, norm_gain, w_query, w_key, w_value)
        inv_rms, unit_rows, normed, key_input, query_heads, key_heads, value_heads, attn_prob, attn_half, attended = parts
        grad_in = incoming + take(mem_cot, owner).astype(jnp.float32)
        passed, out_grad, att_heads, score_grad, query_grad, gain_term = chain_part(grad_in, take(slot_used, owner).astype(jnp.float32), unit_rows, inv_rms, attn_prob, key_heads, value_heads, norm_gain, w_query, w_out)
        weight_terms = weight_part(normed, key_input, query_heads, attn_half, attended, out_grad, att_heads, score_grad, query_grad)
        return ((passed, sum_query + weight_terms[0], sum_key + weight_terms[1], sum_value + weight_terms[2], sum_out + weight_terms[3], sum_gain + gain_term), passed)
    zero_square = jnp.zeros((features, features), jnp.float32)
    start = (jnp.zeros((batch, row_count, features), jnp.float32), zero_square, zero_square, zero_square, zero_square, jnp.zeros((features,), jnp.float32))
    owner_order = jnp.arange(owners - 1, -1, -1, dtype=jnp.int32)
    final, stacked = lax.scan(one_clip, start, owner_order)
    grad_memory = jnp.flip(stacked, 0).reshape(owners, groups, streams, row_count, features).transpose(1, 0, 2, 3, 4)
    mean_scale = 1.0 / (groups * owners * streams)
    return (grad_memory, final[1] * mean_scale, final[2] * mean_scale, final[3] * mean_scale, final[4] * mean_scale, final[5] * mean_scale)
```

```python
import functools
import math

import jax
import jax.numpy as jnp
from jax import lax
from jax.experimental import pallas as pl
from jax.experimental.pallas import tpu as pltpu
from jax.sharding import PartitionSpec as P

NORM_EPSILON = 1e-06
MESH = pl.DeviceIdType.MESH
F32 = jnp.float32
BF16 = jnp.bfloat16
NN = (((1,), (0,)), ((), ()))
NT = (((1,), (1,)), ((), ()))
TN = (((0,), (0,)), ((), ()))
CHUNKS = 2


def dot(left, right, form):
    return lax.dot_general(left, right, form, preferred_element_type=F32)


def key_rows(frame_rows, offset, position):
    length, features = frame_rows.shape
    within = jnp.arange(length, dtype=jnp.int32)
    frame_time = (offset + position * length + within).astype(F32)
    half_width = features // 2
    frequency = 0.0625 * jnp.exp(-math.log(1000.0) * jnp.arange(half_width, dtype=F32) / half_width)
    phases = frame_time[:, None] * frequency
    return frame_rows + jnp.concatenate([jnp.sin(phases), jnp.cos(phases)], axis=-1)


def group_member(groups, g):
    me = lax.axis_index("tm")
    return {"video": lax.div(g, 2), "tm": (me // 2) * 2 + lax.rem(g, 2)}


def chain_kernel(
    owners, groups, heads,
    slot_ref, mem_ref, keyin_ref, cot_ref, bias_ref, gain_ref, wq_ref, wk_ref, wv_ref, wo_ref,
    grad_ref, a1_ref, a2_ref, b1_ref, b2_ref, gsum_ref,
    incoming, mine, prob, half, kbd, vbd, qp, att_all, sg_all, og_all, qg_all, unit_ref, inv_ref,
    chain_send, chain_recv, a_send, a_recv,
):
    me = lax.axis_index("tm")
    vid = lax.axis_index("video")
    rows, features = mem_ref.shape
    length = keyin_ref.shape[0]
    head = features // heads
    pairs = heads // 2
    pw = 2 * head
    members = 2 * groups
    g_me = vid * 2 + lax.rem(me, 2)
    scale = head ** (-0.5)

    barrier = pltpu.get_barrier_semaphore()
    for off in range(1, members):
        pl.semaphore_signal(barrier, inc=1, device_id=group_member(groups, lax.rem(g_me + off, members)), device_id_type=MESH)

    @pl.when(me > 0)
    def _():
        pl.semaphore_signal(barrier, inc=1, device_id={"tm": me - 1}, device_id_type=MESH)

    @pl.when(me < owners - 1)
    def _():
        pl.semaphore_signal(barrier, inc=1, device_id={"tm": me + 1}, device_id_type=MESH)

    ends = jnp.where(me > 0, 1, 0) + jnp.where(me < owners - 1, 1, 0)
    pl.semaphore_wait(barrier, members - 1 + ends)

    def a_copy(which, src, dst, off):
        g = lax.rem(g_me + off, members)
        return pltpu.make_async_remote_copy(
            src_ref=src, dst_ref=dst.at[g_me], send_sem=a_send.at[which, off], recv_sem=a_recv.at[which, g_me],
            device_id=group_member(groups, g), device_id_type=MESH,
        )

    for off in range(1, members):
        a_copy(0, keyin_ref, a1_ref, off).start()
    a1_ref[g_me] = keyin_ref[...]

    mem = mem_ref[...].astype(F32)
    inv = lax.rsqrt(jnp.mean(mem * mem, axis=-1, keepdims=True) + NORM_EPSILON)
    unit = mem * inv
    unit_ref[...] = unit
    inv_ref[...] = jnp.broadcast_to(inv, inv_ref.shape)
    normed = (unit * gain_ref[...]).astype(BF16)
    mine[1] = normed.astype(F32)
    keyin = keyin_ref[...].astype(BF16)
    qp[...] = dot(normed, wq_ref[...], NN).astype(BF16)
    kp = dot(keyin, wk_ref[...], NN).astype(BF16)
    vp = dot(keyin, wv_ref[...], NN).astype(BF16)
    low = lax.broadcasted_iota(jnp.int32, (length, pw), 1) < head
    zero = jnp.zeros((length, pw), BF16)
    for p in range(pairs):
        kk = kp[:, p * pw:(p + 1) * pw]
        vv = vp[:, p * pw:(p + 1) * pw]
        kbd[p, :length] = jnp.where(low, kk, zero)
        kbd[p, length:] = jnp.where(low, zero, kk)
        vbd[p, :length] = jnp.where(low, vv, zero)
        vbd[p, length:] = jnp.where(low, zero, vv)
    for p in range(pairs):
        s2 = dot(qp[:, p * pw:(p + 1) * pw], kbd[p], NT)
        for q in range(2):
            h = 2 * p + q
            s = s2[:, q * length:(q + 1) * length] * scale + bias_ref[h:h + 1, :]
            e = jnp.exp(s - jnp.max(s, axis=-1, keepdims=True))
            pr = e / jnp.sum(e, axis=-1, keepdims=True)
            prob[:, h * length:(h + 1) * length] = pr
            half[:, h * length:(h + 1) * length] = pr.astype(BF16)
        mine[0, :, p * pw:(p + 1) * pw] = dot(half[:, p * 2 * length:(p + 1) * 2 * length], vbd[p], NN).astype(BF16).astype(F32)

    for off in range(1, members):
        g = lax.rem(g_me + off, members)
        a_copy(1, mine.at[lax.rem(g, 2)], a2_ref, off).start()
    a2_ref[g_me] = mine[lax.rem(me, 2)]

    live = slot_ref[0].astype(F32)
    step = rows // CHUNKS

    def chain_copy(c):
        return pltpu.make_async_remote_copy(
            src_ref=grad_ref.at[pl.ds(c * step, step)], dst_ref=incoming.at[pl.ds(c * step, step)],
            send_sem=chain_send.at[c], recv_sem=chain_recv.at[c],
            device_id={"tm": jnp.maximum(me - 1, 0)}, device_id_type=MESH,
        )

    @pl.when(me == owners - 1)
    def _():
        incoming[...] = jnp.zeros_like(incoming)

    gain_total = jnp.zeros((1, features), F32)
    for c in range(CHUNKS):
        r = slice(c * step, (c + 1) * step)

        @pl.when(me < owners - 1)
        def _():
            chain_copy(c).wait_recv()

        grad_in = incoming[r, :] + cot_ref[r, :].astype(F32)
        og = (live * grad_in).astype(BF16)
        og_all[r, :] = og
        att = dot(og, wo_ref[...], NT).astype(BF16)
        att_all[r, :] = att
        for p in range(pairs):
            pg2 = dot(att[:, p * pw:(p + 1) * pw], vbd[p], NT)
            for q in range(2):
                h = 2 * p + q
                pg = pg2[:, q * length:(q + 1) * length]
                pr = prob[r, h * length:(h + 1) * length]
                inner = jnp.sum(pr * pg, axis=-1, keepdims=True)
                sg_all[r, h * length:(h + 1) * length] = (pr * (pg - inner) * scale).astype(BF16)
            qg_all[r, p * pw:(p + 1) * pw] = dot(sg_all[r, p * 2 * length:(p + 1) * 2 * length], kbd[p], NN).astype(BF16)
        ng = dot(qg_all[r, :], wq_ref[...], NT)
        un = unit_ref[r, :]
        gain_total = gain_total + jnp.sum(ng * un, axis=0, keepdims=True)
        sc = ng * gain_ref[...]
        grad_ref[r, :] = grad_in + inv_ref[r, 0:1] * (sc - un * jnp.mean(sc * un, axis=-1, keepdims=True))

        @pl.when(me > 0)
        def _():
            chain_copy(c).start()

    gsum_ref[...] = gain_total

    width = features // groups
    lowr = lax.broadcasted_iota(jnp.int32, (rows, pw), 1) < head
    zr = jnp.zeros((rows, pw), BF16)

    def put(out, which, p, value):
        for v in range(groups):
            lo, hi = max(p * pw, v * width), min((p + 1) * pw, (v + 1) * width)
            if lo < hi:
                out[which, v, :, lo - v * width:hi - v * width] = value[:, lo - p * pw:hi - p * pw]

    for p in range(pairs):
        for which, (left_ref, right_ref) in enumerate(((sg_all, qp), (half, att_all))):
            right = right_ref[:, p * pw:(p + 1) * pw]
            right = jnp.concatenate([jnp.where(lowr, right, zr), jnp.where(lowr, zr, right)], axis=0)
            base = 2 * p * length
            left = jnp.concatenate([left_ref[:, base:base + length], left_ref[:, base + length:base + 2 * length]], axis=0)
            put(b1_ref, which, p, dot(left, right, TN).astype(BF16).astype(F32))
        put(b2_ref, 0, p, og_all[:, p * pw:(p + 1) * pw].astype(F32))
        put(b2_ref, 1, p, qg_all[:, p * pw:(p + 1) * pw].astype(F32))

    @pl.when(me > 0)
    def _():
        for c in range(CHUNKS):
            chain_copy(c).wait_send()

    for off in range(1, members):
        g = lax.rem(g_me + members - off, members)
        for which, dst in ((0, a1_ref), (1, a2_ref)):
            a_copy(which, dst.at[g_me], dst, off).wait_send()
            pltpu.make_async_remote_copy(
                src_ref=dst.at[g], dst_ref=dst.at[g], send_sem=a_send.at[which, off], recv_sem=a_recv.at[which, g],
                device_id=group_member(groups, g), device_id_type=MESH,
            ).wait_recv()


def reduce_kernel(
    owners, groups,
    a1_ref, a2_ref, b1_ref, b2_ref, gsum_ref,
    out_ref, gain_ref,
    s1, s2, t1, t2, acc, final, gslot, gquad, *rest,
):
    me = lax.axis_index("tm")
    vid = lax.axis_index("video")
    members = 2 * groups
    chips = owners // 2
    bits = chips.bit_length() - 1
    lands = rest[:bits]
    b_send, b_recv, r_send, r_recv, q_send, q_recv, f_send, f_recv = rest[bits:]
    chip, core = me // 2, lax.rem(me, 2)
    g_me = vid * 2 + core
    pieces, features, pw = acc.shape
    per = pieces // 2
    block = features // chips
    part = block // 2
    scale = 1.0 / (owners * groups)

    barrier = pltpu.get_barrier_semaphore()
    for off in range(1, members):
        pl.semaphore_signal(barrier, inc=1, device_id=group_member(groups, lax.rem(g_me + off, members)), device_id_type=MESH)
    for off in range(1, chips):
        pl.semaphore_signal(barrier, inc=1, device_id={"tm": lax.rem(me + 2 * off, owners)}, device_id_type=MESH)
    pl.semaphore_wait(barrier, members - 1 + chips - 1)

    def b_copy(which, off):
        g = lax.rem(g_me + off, members)
        v, c = lax.div(g, 2), lax.rem(g, 2)
        src, dst = ((b1_ref.at[c, v], s1), (b2_ref.at[c, v], s2), (gsum_ref, gslot))[which]
        return pltpu.make_async_remote_copy(
            src_ref=src, dst_ref=dst.at[g_me], send_sem=b_send.at[which, off], recv_sem=b_recv.at[which, g_me],
            device_id=group_member(groups, g), device_id_type=MESH,
        )

    def b_arrive(which, off):
        g = lax.rem(g_me + members - off, members)
        dst = (s1, s2, gslot)[which]
        return pltpu.make_async_remote_copy(
            src_ref=dst.at[g], dst_ref=dst.at[g], send_sem=b_send.at[which, off], recv_sem=b_recv.at[which, g],
            device_id=group_member(groups, g), device_id_type=MESH,
        )

    for which in (2, 1, 0):
        for off in range(1, members):
            b_copy(which, off).start()
    s1[g_me] = b1_ref[core, vid]
    s2[g_me] = b2_ref[core, vid]
    gslot[g_me] = gsum_ref[...]
    for g in range(members):
        t1[g] = a1_ref[g].astype(BF16)
        t2[g] = a2_ref[g].astype(BF16)

    order = [int(format(i, "b").zfill(bits)[::-1], 2) if bits else 0 for i in range(chips)]

    def products(which):
        slots, left = ((s2, t2), (s1, t1))[which]
        for off in range(1, members):
            b_arrive(1 - which, off).wait_recv()
        flat = left[...].reshape(members * left.shape[1], features)
        for i in range(per):
            right = slots[:, :, i * pw:(i + 1) * pw].reshape(flat.shape[0], pw).astype(BF16)
            value = dot(flat, right, TN)
            for pos in range(chips):
                k = order[pos]
                acc[which * per + i, pos * block:(pos + 1) * block, :] = value[k * block:(k + 1) * block, :]

    starts = []
    lo = 0
    for s in range(bits):
        span = features >> (s + 1)
        bit = lax.rem(lax.div(chip, 2 ** s), 2)
        starts.append((lo + (1 - bit) * span, lo + bit * span, span, chip + (1 - 2 * bit) * 2 ** s))
        lo = lo + bit * span
    home = pl.multiple_of(lo, 8)

    def r_copy(p, s):
        give, _, span, peer = starts[s]
        return pltpu.make_async_remote_copy(
            src_ref=acc.at[p, pl.ds(pl.multiple_of(give, 8), span)], dst_ref=lands[s].at[p],
            send_sem=r_send.at[p, s], recv_sem=r_recv.at[p, s],
            device_id={"tm": peer * 2 + core}, device_id_type=MESH,
        )

    def r_finish(p, s):
        _, keep, span, _ = starts[s]
        r_copy(p, s).wait_recv()
        at = pl.ds(pl.multiple_of(keep, 8), span)
        acc[p, at, :] = acc[p, at, :] + lands[s][p]

    def f_copy(p):
        theirs = pl.ds(pl.multiple_of(lo + (1 - core) * part, 8), part)
        return pltpu.make_async_remote_copy(
            src_ref=acc.at[p, theirs], dst_ref=final.at[p], send_sem=f_send.at[p], recv_sem=f_recv.at[p],
            device_id={"tm": chip * 2 + 1 - core}, device_id_type=MESH,
        )

    for wave in range(pieces + bits):
        if wave == 0:
            products(0)
        if wave == per:
            products(1)
        for s in reversed(range(bits + 1)):
            p = wave - s
            if 0 <= p < pieces:
                if s > 0:
                    r_finish(p, s - 1)
                if s < bits:
                    r_copy(p, s).start()
                else:
                    f_copy(p).start()
        if wave == 0:
            for off in range(1, members):
                b_arrive(2, off).wait_recv()
            gquad[chip] = jnp.sum(gslot[...], axis=0)
            for off in range(1, chips):
                g_copy = pltpu.make_async_remote_copy(
                    src_ref=gquad.at[chip], dst_ref=gquad.at[chip], send_sem=q_send.at[off], recv_sem=q_recv.at[chip],
                    device_id={"tm": lax.rem(me + 2 * off, owners)}, device_id_type=MESH,
                )
                g_copy.start()

    mine_rows = pl.ds(pl.multiple_of(lo + core * part, 8), part)
    for p in range(pieces):
        which, i = p // per, p % per
        cols = slice(i * pw, (i + 1) * pw)
        out_ref[2 * which + core, :, cols] = acc[p, mine_rows, :] * scale
    for p in range(pieces):
        which, i = p // per, p % per
        cols = slice(i * pw, (i + 1) * pw)
        f_copy(p).wait_recv()
        out_ref[2 * which + 1 - core, :, cols] = final[p] * scale

    for off in range(1, chips):
        src = lax.rem(chip + chips - off, chips)
        got = pltpu.make_async_remote_copy(
            src_ref=gquad.at[src], dst_ref=gquad.at[src], send_sem=q_send.at[off], recv_sem=q_recv.at[src],
            device_id={"tm": lax.rem(me + 2 * off, owners)}, device_id_type=MESH,
        )
        got.wait()
    gain_ref[...] = jnp.sum(gquad[...], axis=0) * scale
    for which in range(3):
        for off in range(1, members):
            b_copy(which, off).wait_send()
    for p in range(pieces):
        for s in range(bits):
            r_copy(p, s).wait_send()
        f_copy(p).wait_send()


def on_device(
    memory, frames, mem_cot, slot_used, key_bias, start_offset, norm_gain, w_query, w_key, w_value, w_out
):
    owners = lax.axis_size("tm")
    groups = lax.axis_size("video")
    position = lax.axis_index("tm")
    streams, rows, features = memory.shape[2:]
    length = frames.shape[3]
    heads = key_bias.shape[3]
    members = 2 * groups
    chips = owners // 2
    bits = chips.bit_length() - 1
    width = features // groups
    keyin = key_rows(frames[0, 0, 0], start_offset[0, 0], position)
    vmem = pl.BlockSpec(memory_space=pltpu.VMEM)
    smem = pl.BlockSpec(memory_space=pltpu.SMEM)
    sds = jax.ShapeDtypeStruct
    grad, a1, a2, b1, b2, gsum = pl.pallas_call(
        functools.partial(chain_kernel, owners, groups, heads),
        out_shape=(
            sds((rows, features), F32),
            sds((members, length, features), F32),
            sds((members, rows, features), F32),
            sds((2, groups, length, width), F32),
            sds((2, groups, rows, width), F32),
            sds((1, features), F32),
        ),
        in_specs=[smem] + [vmem] * 9,
        out_specs=(vmem,) * 6,
        scratch_shapes=[
            pltpu.VMEM((rows, features), F32),
            pltpu.VMEM((2, rows, features), F32),
            pltpu.VMEM((rows, heads * length), F32),
            pltpu.VMEM((rows, heads * length), BF16),
            pltpu.VMEM((heads // 2, 2 * length, 2 * features // heads), BF16),
            pltpu.VMEM((heads // 2, 2 * length, 2 * features // heads), BF16),
            pltpu.VMEM((rows, features), BF16),
            pltpu.VMEM((rows, features), BF16),
            pltpu.VMEM((rows, heads * length), BF16),
            pltpu.VMEM((rows, features), BF16),
            pltpu.VMEM((rows, features), BF16),
            pltpu.VMEM((rows, features), F32),
            pltpu.VMEM((rows, 128), F32),
            pltpu.SemaphoreType.DMA((CHUNKS,)),
            pltpu.SemaphoreType.DMA((CHUNKS,)),
            pltpu.SemaphoreType.DMA((2, members)),
            pltpu.SemaphoreType.DMA((2, members)),
        ],
        compiler_params=pltpu.CompilerParams(collective_id=0, has_side_effects=True, vmem_limit_bytes=56 * 1024 * 1024),
        name="chain",
    )(
        slot_used[0, 0], memory[0, 0, 0], keyin, mem_cot[0, 0, 0], key_bias[0, 0, 0],
        norm_gain[None, :], w_query, w_key, w_value, w_out,
    )
    pw = 128 if width % 128 == 0 else width
    pieces = 2 * (width // pw)
    dma = pltpu.SemaphoreType.DMA
    weights, gain = pl.pallas_call(
        functools.partial(reduce_kernel, owners, groups),
        out_shape=(sds((4, features // owners, width), F32), sds((1, features), F32)),
        in_specs=[vmem] * 5,
        out_specs=(vmem,) * 2,
        scratch_shapes=[
            pltpu.VMEM((members, length, width), F32),
            pltpu.VMEM((members, rows, width), F32),
            pltpu.VMEM((members, length, features), BF16),
            pltpu.VMEM((members, rows, features), BF16),
            pltpu.VMEM((pieces, features, pw), F32),
            pltpu.VMEM((pieces, features // owners, pw), F32),
            pltpu.VMEM((members, 1, features), F32),
            pltpu.VMEM((chips, 1, features), F32),
        ]
        + [pltpu.VMEM((pieces, features >> (s + 1), pw), F32) for s in range(bits)]
        + [
            dma((3, members)), dma((3, members)), dma((pieces, bits)), dma((pieces, bits)),
            dma((chips,)), dma((chips,)), dma((pieces,)), dma((pieces,)),
        ],
        compiler_params=pltpu.CompilerParams(collective_id=1, has_side_effects=True, vmem_limit_bytes=56 * 1024 * 1024),
        name="reduce",
    )(a1, a2, b1, b2, gsum)
    return (grad[None, None, None], weights[1], weights[2], weights[3], weights[0], gain[0])


def solution(mesh):
    return jax.shard_map(
        on_device,
        mesh=mesh,
        in_specs=(
            P("video", "tm", None, None, None),
            P("video", "tm", None, None, None),
            P("video", "tm", None, None, None),
            P("video", "tm", None),
            P("video", "tm", None, None, None),
            P("video", None),
            P(),
            P(),
            P(),
            P(),
            P(),
        ),
        out_specs=(
            P("video", "tm", None, None, None),
            P("tm", "video"),
            P("tm", "video"),
            P("tm", "video"),
            P("tm", "video"),
            P(),
        ),
        check_vma=False,
    )
```

```python
import functools
import math

import jax
import jax.numpy as jnp
from jax import lax
from jax.experimental import pallas as pl
from jax.experimental.pallas import tpu as pltpu
from jax.sharding import PartitionSpec as P

NORM_EPSILON = 1e-06
MESH = pl.DeviceIdType.MESH
F32 = jnp.float32
BF16 = jnp.bfloat16
NN = (((1,), (0,)), ((), ()))
NT = (((1,), (1,)), ((), ()))
TN = (((0,), (0,)), ((), ()))
CHUNKS = 4


def dot(left, right, form):
    return lax.dot_general(left, right, form, preferred_element_type=F32)


def key_rows(frame_rows, offset, position):
    length, features = frame_rows.shape
    within = jnp.arange(length, dtype=jnp.int32)
    frame_time = (offset + position * length + within).astype(F32)
    half_width = features // 2
    frequency = 0.0625 * jnp.exp(-math.log(1000.0) * jnp.arange(half_width, dtype=F32) / half_width)
    phases = frame_time[:, None] * frequency
    return frame_rows + jnp.concatenate([jnp.sin(phases), jnp.cos(phases)], axis=-1)


def group_member(groups, g):
    me = lax.axis_index("tm")
    return {"video": lax.div(g, 2), "tm": (me // 2) * 2 + lax.rem(g, 2)}


def chain_kernel(
    owners, groups, heads,
    slot_ref, mem_ref, keyin_ref, cot_ref, bias_ref, gain_ref, wq_ref, wk_ref, wv_ref, wo_ref,
    grad_ref, a1_ref, a2_ref, b1_ref, b2_ref, gsum_ref,
    incoming, mine, prob, half, kbd, vbd, qp, att_all, sg_all, og_all, qg_all, unit_ref, inv_ref,
    chain_send, chain_recv, a_send, a_recv,
):
    me = lax.axis_index("tm")
    vid = lax.axis_index("video")
    rows, features = mem_ref.shape
    length = keyin_ref.shape[0]
    head = features // heads
    pairs = heads // 2
    pw = 2 * head
    members = 2 * groups
    g_me = vid * 2 + lax.rem(me, 2)
    scale = head ** (-0.5)

    barrier = pltpu.get_barrier_semaphore()
    for off in range(1, members):
        pl.semaphore_signal(barrier, inc=1, device_id=group_member(groups, lax.rem(g_me + off, members)), device_id_type=MESH)

    @pl.when(me > 0)
    def _():
        pl.semaphore_signal(barrier, inc=1, device_id={"tm": me - 1}, device_id_type=MESH)

    @pl.when(me < owners - 1)
    def _():
        pl.semaphore_signal(barrier, inc=1, device_id={"tm": me + 1}, device_id_type=MESH)

    ends = jnp.where(me > 0, 1, 0) + jnp.where(me < owners - 1, 1, 0)
    pl.semaphore_wait(barrier, members - 1 + ends)

    def a_copy(which, src, dst, off):
        g = lax.rem(g_me + off, members)
        return pltpu.make_async_remote_copy(
            src_ref=src, dst_ref=dst.at[g_me], send_sem=a_send.at[which, off], recv_sem=a_recv.at[which, g_me],
            device_id=group_member(groups, g), device_id_type=MESH,
        )

    for off in range(1, members):
        a_copy(0, keyin_ref, a1_ref, off).start()
    a1_ref[g_me] = keyin_ref[...]

    mem = mem_ref[...].astype(F32)
    inv = lax.rsqrt(jnp.mean(mem * mem, axis=-1, keepdims=True) + NORM_EPSILON)
    unit = mem * inv
    unit_ref[...] = unit
    inv_ref[...] = jnp.broadcast_to(inv, inv_ref.shape)
    normed = (unit * gain_ref[...]).astype(BF16)
    mine[1] = normed.astype(F32)
    keyin = keyin_ref[...].astype(BF16)
    qp[...] = dot(normed, wq_ref[...], NN).astype(BF16)
    kp = dot(keyin, wk_ref[...], NN).astype(BF16)
    vp = dot(keyin, wv_ref[...], NN).astype(BF16)
    low = lax.broadcasted_iota(jnp.int32, (length, pw), 1) < head
    zero = jnp.zeros((length, pw), BF16)
    for p in range(pairs):
        kk = kp[:, p * pw:(p + 1) * pw]
        vv = vp[:, p * pw:(p + 1) * pw]
        kbd[p, :length] = jnp.where(low, kk, zero)
        kbd[p, length:] = jnp.where(low, zero, kk)
        vbd[p, :length] = jnp.where(low, vv, zero)
        vbd[p, length:] = jnp.where(low, zero, vv)
    for p in range(pairs):
        s2 = dot(qp[:, p * pw:(p + 1) * pw], kbd[p], NT)
        for q in range(2):
            h = 2 * p + q
            s = s2[:, q * length:(q + 1) * length] * scale + bias_ref[h:h + 1, :]
            e = jnp.exp(s - jnp.max(s, axis=-1, keepdims=True))
            pr = e / jnp.sum(e, axis=-1, keepdims=True)
            prob[:, h * length:(h + 1) * length] = pr
            half[:, h * length:(h + 1) * length] = pr.astype(BF16)
        mine[0, :, p * pw:(p + 1) * pw] = dot(half[:, p * 2 * length:(p + 1) * 2 * length], vbd[p], NN).astype(BF16).astype(F32)

    for off in range(1, members):
        g = lax.rem(g_me + off, members)
        a_copy(1, mine.at[lax.rem(g, 2)], a2_ref, off).start()
    a2_ref[g_me] = mine[lax.rem(me, 2)]

    live = slot_ref[0].astype(F32)
    step = rows // CHUNKS

    def chain_copy(c):
        return pltpu.make_async_remote_copy(
            src_ref=grad_ref.at[pl.ds(c * step, step)], dst_ref=incoming.at[pl.ds(c * step, step)],
            send_sem=chain_send.at[c], recv_sem=chain_recv.at[c],
            device_id={"tm": jnp.maximum(me - 1, 0)}, device_id_type=MESH,
        )

    @pl.when(me == owners - 1)
    def _():
        incoming[...] = jnp.zeros_like(incoming)

    gain_total = jnp.zeros((1, features), F32)
    for c in range(CHUNKS):
        r = slice(c * step, (c + 1) * step)

        @pl.when(me < owners - 1)
        def _():
            chain_copy(c).wait_recv()

        grad_in = incoming[r, :] + cot_ref[r, :].astype(F32)
        og = (live * grad_in).astype(BF16)
        og_all[r, :] = og
        att = dot(og, wo_ref[...], NT).astype(BF16)
        att_all[r, :] = att
        for p in range(pairs):
            pg2 = dot(att[:, p * pw:(p + 1) * pw], vbd[p], NT)
            for q in range(2):
                h = 2 * p + q
                pg = pg2[:, q * length:(q + 1) * length]
                pr = prob[r, h * length:(h + 1) * length]
                inner = jnp.sum(pr * pg, axis=-1, keepdims=True)
                sg_all[r, h * length:(h + 1) * length] = (pr * (pg - inner) * scale).astype(BF16)
            qg_all[r, p * pw:(p + 1) * pw] = dot(sg_all[r, p * 2 * length:(p + 1) * 2 * length], kbd[p], NN).astype(BF16)
        ng = dot(qg_all[r, :], wq_ref[...], NT)
        un = unit_ref[r, :]
        gain_total = gain_total + jnp.sum(ng * un, axis=0, keepdims=True)
        sc = ng * gain_ref[...]
        grad_ref[r, :] = grad_in + inv_ref[r, 0:1] * (sc - un * jnp.mean(sc * un, axis=-1, keepdims=True))

        @pl.when(me > 0)
        def _():
            chain_copy(c).start()

    gsum_ref[...] = gain_total

    width = features // groups
    lowr = lax.broadcasted_iota(jnp.int32, (rows, pw), 1) < head
    zr = jnp.zeros((rows, pw), BF16)

    def put(out, which, p, value):
        for v in range(groups):
            lo, hi = max(p * pw, v * width), min((p + 1) * pw, (v + 1) * width)
            if lo < hi:
                out[which, v, :, lo - v * width:hi - v * width] = value[:, lo - p * pw:hi - p * pw]

    for p in range(pairs):
        for which, (left_ref, right_ref) in enumerate(((sg_all, qp), (half, att_all))):
            right = right_ref[:, p * pw:(p + 1) * pw]
            right = jnp.concatenate([jnp.where(lowr, right, zr), jnp.where(lowr, zr, right)], axis=0)
            base = 2 * p * length
            left = jnp.concatenate([left_ref[:, base:base + length], left_ref[:, base + length:base + 2 * length]], axis=0)
            put(b1_ref, which, p, dot(left, right, TN).astype(BF16).astype(F32))
        put(b2_ref, 0, p, og_all[:, p * pw:(p + 1) * pw].astype(F32))
        put(b2_ref, 1, p, qg_all[:, p * pw:(p + 1) * pw].astype(F32))

    @pl.when(me > 0)
    def _():
        for c in range(CHUNKS):
            chain_copy(c).wait_send()

    for off in range(1, members):
        g = lax.rem(g_me + members - off, members)
        for which, dst in ((0, a1_ref), (1, a2_ref)):
            a_copy(which, dst.at[g_me], dst, off).wait_send()
            pltpu.make_async_remote_copy(
                src_ref=dst.at[g], dst_ref=dst.at[g], send_sem=a_send.at[which, off], recv_sem=a_recv.at[which, g],
                device_id=group_member(groups, g), device_id_type=MESH,
            ).wait_recv()


def reduce_kernel(
    owners, groups,
    a1_ref, a2_ref, b1_ref, b2_ref, gsum_ref,
    out_ref, gain_ref,
    s1, s2, t1, t2, acc, final, gslot, gquad, *rest,
):
    me = lax.axis_index("tm")
    vid = lax.axis_index("video")
    members = 2 * groups
    chips = owners // 2
    bits = chips.bit_length() - 1
    lands = rest[:bits]
    b_send, b_recv, r_send, r_recv, q_send, q_recv, f_send, f_recv = rest[bits:]
    chip, core = me // 2, lax.rem(me, 2)
    g_me = vid * 2 + core
    pieces, features, pw = acc.shape
    per = pieces // 2
    block = features // chips
    part = block // 2
    scale = 1.0 / (owners * groups)
    length, rows = a1_ref.shape[1], a2_ref.shape[1]

    barrier = pltpu.get_barrier_semaphore()
    for off in range(1, members):
        pl.semaphore_signal(barrier, inc=1, device_id=group_member(groups, lax.rem(g_me + off, members)), device_id_type=MESH)
    for off in range(1, chips):
        pl.semaphore_signal(barrier, inc=1, device_id={"tm": lax.rem(me + 2 * off, owners)}, device_id_type=MESH)
    pl.semaphore_wait(barrier, members - 1 + chips - 1)

    def b_copy(which, off):
        g = lax.rem(g_me + off, members)
        v, c = lax.div(g, 2), lax.rem(g, 2)
        src, dst = ((b1_ref.at[c, v], s1), (b2_ref.at[c, v], s2), (gsum_ref, gslot))[which]
        return pltpu.make_async_remote_copy(
            src_ref=src, dst_ref=dst.at[g_me], send_sem=b_send.at[which, off], recv_sem=b_recv.at[which, g_me],
            device_id=group_member(groups, g), device_id_type=MESH,
        )

    def b_arrive(which, off):
        g = lax.rem(g_me + members - off, members)
        dst = (s1, s2, gslot)[which]
        return pltpu.make_async_remote_copy(
            src_ref=dst.at[g], dst_ref=dst.at[g], send_sem=b_send.at[which, off], recv_sem=b_recv.at[which, g],
            device_id=group_member(groups, g), device_id_type=MESH,
        )

    for which in (2, 1, 0):
        for off in range(1, members):
            b_copy(which, off).start()
    s1[g_me] = b1_ref[core, vid]
    s2[g_me] = b2_ref[core, vid]
    gslot[g_me] = gsum_ref[...]
    for g in range(members):
        t1[:, g * length:(g + 1) * length] = jnp.transpose(a1_ref[g]).astype(BF16)
    for g in range(0, members, 2):
        both = jnp.concatenate([a2_ref[g], a2_ref[g + 1]], axis=0)
        t2[:, g * rows:(g + 2) * rows] = jnp.transpose(both).astype(BF16)

    order = [int(format(i, "b").zfill(bits)[::-1], 2) if bits else 0 for i in range(chips)]

    def products(which):
        slots, left = ((s2, t2), (s1, t1))[which]
        for off in range(1, members):
            b_arrive(1 - which, off).wait_recv()
        for i in range(per):
            right = slots[:, :, i * pw:(i + 1) * pw].reshape(left.shape[1], pw).astype(BF16)
            value = dot(left[...], right, NN)
            for pos in range(chips):
                k = order[pos]
                acc[which * per + i, pos * block:(pos + 1) * block, :] = value[k * block:(k + 1) * block, :]

    starts = []
    lo = 0
    for s in range(bits):
        span = features >> (s + 1)
        bit = lax.rem(lax.div(chip, 2 ** s), 2)
        starts.append((lo + (1 - bit) * span, lo + bit * span, span, chip + (1 - 2 * bit) * 2 ** s))
        lo = lo + bit * span
    home = pl.multiple_of(lo, 8)

    def r_copy(p, s):
        give, _, span, peer = starts[s]
        return pltpu.make_async_remote_copy(
            src_ref=acc.at[p, pl.ds(pl.multiple_of(give, 8), span)], dst_ref=lands[s].at[p],
            send_sem=r_send.at[p, s], recv_sem=r_recv.at[p, s],
            device_id={"tm": peer * 2 + core}, device_id_type=MESH,
        )

    def r_finish(p, s):
        _, keep, span, _ = starts[s]
        r_copy(p, s).wait_recv()
        at = pl.ds(pl.multiple_of(keep, 8), span)
        acc[p, at, :] = acc[p, at, :] + lands[s][p]

    def f_copy(p):
        theirs = pl.ds(pl.multiple_of(lo + (1 - core) * part, 8), part)
        return pltpu.make_async_remote_copy(
            src_ref=acc.at[p, theirs], dst_ref=final.at[p], send_sem=f_send.at[p], recv_sem=f_recv.at[p],
            device_id={"tm": chip * 2 + 1 - core}, device_id_type=MESH,
        )

    for wave in range(pieces + bits):
        if wave == 0:
            products(0)
        if wave == per:
            products(1)
        for s in reversed(range(bits + 1)):
            p = wave - s
            if 0 <= p < pieces:
                if s > 0:
                    r_finish(p, s - 1)
                if s < bits:
                    r_copy(p, s).start()
                else:
                    f_copy(p).start()
        if wave == 0:
            for off in range(1, members):
                b_arrive(2, off).wait_recv()
            gquad[chip] = jnp.sum(gslot[...], axis=0)
            for off in range(1, chips):
                g_copy = pltpu.make_async_remote_copy(
                    src_ref=gquad.at[chip], dst_ref=gquad.at[chip], send_sem=q_send.at[off], recv_sem=q_recv.at[chip],
                    device_id={"tm": lax.rem(me + 2 * off, owners)}, device_id_type=MESH,
                )
                g_copy.start()

    mine_rows = pl.ds(pl.multiple_of(lo + core * part, 8), part)
    for p in range(pieces):
        which, i = p // per, p % per
        cols = slice(i * pw, (i + 1) * pw)
        out_ref[2 * which + core, :, cols] = acc[p, mine_rows, :] * scale
    for p in range(pieces):
        which, i = p // per, p % per
        cols = slice(i * pw, (i + 1) * pw)
        f_copy(p).wait_recv()
        out_ref[2 * which + 1 - core, :, cols] = final[p] * scale

    for off in range(1, chips):
        src = lax.rem(chip + chips - off, chips)
        got = pltpu.make_async_remote_copy(
            src_ref=gquad.at[src], dst_ref=gquad.at[src], send_sem=q_send.at[off], recv_sem=q_recv.at[src],
            device_id={"tm": lax.rem(me + 2 * off, owners)}, device_id_type=MESH,
        )
        got.wait()
    gain_ref[...] = jnp.sum(gquad[...], axis=0) * scale
    for which in range(3):
        for off in range(1, members):
            b_copy(which, off).wait_send()
    for p in range(pieces):
        for s in range(bits):
            r_copy(p, s).wait_send()
        f_copy(p).wait_send()


def on_device(
    memory, frames, mem_cot, slot_used, key_bias, start_offset, norm_gain, w_query, w_key, w_value, w_out
):
    owners = lax.axis_size("tm")
    groups = lax.axis_size("video")
    position = lax.axis_index("tm")
    streams, rows, features = memory.shape[2:]
    length = frames.shape[3]
    heads = key_bias.shape[3]
    members = 2 * groups
    chips = owners // 2
    bits = chips.bit_length() - 1
    width = features // groups
    keyin = key_rows(frames[0, 0, 0], start_offset[0, 0], position)
    vmem = pl.BlockSpec(memory_space=pltpu.VMEM)
    smem = pl.BlockSpec(memory_space=pltpu.SMEM)
    sds = jax.ShapeDtypeStruct
    grad, a1, a2, b1, b2, gsum = pl.pallas_call(
        functools.partial(chain_kernel, owners, groups, heads),
        out_shape=(
            sds((rows, features), F32),
            sds((members, length, features), F32),
            sds((members, rows, features), F32),
            sds((2, groups, length, width), F32),
            sds((2, groups, rows, width), F32),
            sds((1, features), F32),
        ),
        in_specs=[smem] + [vmem] * 9,
        out_specs=(vmem,) * 6,
        scratch_shapes=[
            pltpu.VMEM((rows, features), F32),
            pltpu.VMEM((2, rows, features), F32),
            pltpu.VMEM((rows, heads * length), F32),
            pltpu.VMEM((rows, heads * length), BF16),
            pltpu.VMEM((heads // 2, 2 * length, 2 * features // heads), BF16),
            pltpu.VMEM((heads // 2, 2 * length, 2 * features // heads), BF16),
            pltpu.VMEM((rows, features), BF16),
            pltpu.VMEM((rows, features), BF16),
            pltpu.VMEM((rows, heads * length), BF16),
            pltpu.VMEM((rows, features), BF16),
            pltpu.VMEM((rows, features), BF16),
            pltpu.VMEM((rows, features), F32),
            pltpu.VMEM((rows, 128), F32),
            pltpu.SemaphoreType.DMA((CHUNKS,)),
            pltpu.SemaphoreType.DMA((CHUNKS,)),
            pltpu.SemaphoreType.DMA((2, members)),
            pltpu.SemaphoreType.DMA((2, members)),
        ],
        compiler_params=pltpu.CompilerParams(collective_id=0, has_side_effects=True, vmem_limit_bytes=56 * 1024 * 1024),
        name="chain",
    )(
        slot_used[0, 0], memory[0, 0, 0], keyin, mem_cot[0, 0, 0], key_bias[0, 0, 0],
        norm_gain[None, :], w_query, w_key, w_value, w_out,
    )
    pw = 128 if width % 128 == 0 else width
    pieces = 2 * (width // pw)
    dma = pltpu.SemaphoreType.DMA
    weights, gain = pl.pallas_call(
        functools.partial(reduce_kernel, owners, groups),
        out_shape=(sds((4, features // owners, width), F32), sds((1, features), F32)),
        in_specs=[vmem] * 5,
        out_specs=(vmem,) * 2,
        scratch_shapes=[
            pltpu.VMEM((members, length, width), F32),
            pltpu.VMEM((members, rows, width), F32),
            pltpu.VMEM((features, members * length), BF16),
            pltpu.VMEM((features, members * rows), BF16),
            pltpu.VMEM((pieces, features, pw), F32),
            pltpu.VMEM((pieces, features // owners, pw), F32),
            pltpu.VMEM((members, 1, features), F32),
            pltpu.VMEM((chips, 1, features), F32),
        ]
        + [pltpu.VMEM((pieces, features >> (s + 1), pw), F32) for s in range(bits)]
        + [
            dma((3, members)), dma((3, members)), dma((pieces, bits)), dma((pieces, bits)),
            dma((chips,)), dma((chips,)), dma((pieces,)), dma((pieces,)),
        ],
        compiler_params=pltpu.CompilerParams(collective_id=1, has_side_effects=True, vmem_limit_bytes=56 * 1024 * 1024),
        name="reduce",
    )(a1, a2, b1, b2, gsum)
    return (grad[None, None, None], weights[1], weights[2], weights[3], weights[0], gain[0])


def solution(mesh):
    return jax.shard_map(
        on_device,
        mesh=mesh,
        in_specs=(
            P("video", "tm", None, None, None),
            P("video", "tm", None, None, None),
            P("video", "tm", None, None, None),
            P("video", "tm", None),
            P("video", "tm", None, None, None),
            P("video", None),
            P(),
            P(),
            P(),
            P(),
            P(),
        ),
        out_specs=(
            P("video", "tm", None, None, None),
            P("tm", "video"),
            P("tm", "video"),
            P("tm", "video"),
            P("tm", "video"),
            P(),
        ),
        check_vma=False,
    )
```

```python
import functools
import math

import jax
import jax.numpy as jnp
from jax import lax
from jax.experimental import pallas as pl
from jax.experimental.pallas import tpu as pltpu
from jax.sharding import PartitionSpec as P

NORM_EPSILON = 1e-06
MESH = pl.DeviceIdType.MESH
F32 = jnp.float32
BF16 = jnp.bfloat16
NN = (((1,), (0,)), ((), ()))
NT = (((1,), (1,)), ((), ()))
TN = (((0,), (0,)), ((), ()))
CHUNKS = 4


def dot(left, right, form):
    return lax.dot_general(left, right, form, preferred_element_type=F32)


def key_rows(frame_rows, offset, position):
    length, features = frame_rows.shape
    within = jnp.arange(length, dtype=jnp.int32)
    frame_time = (offset + position * length + within).astype(F32)
    half_width = features // 2
    frequency = 0.0625 * jnp.exp(-math.log(1000.0) * jnp.arange(half_width, dtype=F32) / half_width)
    phases = frame_time[:, None] * frequency
    return frame_rows + jnp.concatenate([jnp.sin(phases), jnp.cos(phases)], axis=-1)


def group_member(groups, g):
    me = lax.axis_index("tm")
    return {"video": lax.div(g, 2), "tm": (me // 2) * 2 + lax.rem(g, 2)}


def whole_kernel(
    owners, groups, heads,
    slot_ref, mem_ref, keyin_ref, cot_ref, bias_ref, gain_ref, wq_ref, wk_ref, wv_ref, wo_ref,
    grad_ref, out_ref, gain_out_ref,
    a1_ref, a2_ref, b1_ref, b2_ref, gsum_ref,
    incoming, mine, prob, half, kbd, vbd, qp, att_all, sg_all, og_all, qg_all, unit_ref, inv_ref, wot, wqt,
    chain_send, chain_recv, a_send, a_recv,
    *reduce_scratch,
):
    me = lax.axis_index("tm")
    vid = lax.axis_index("video")
    chips = owners // 2
    bits = chips.bit_length() - 1
    chip, core = me // 2, lax.rem(me, 2)
    peers = [chip + (1 - 2 * lax.rem(lax.div(chip, 2 ** b), 2)) * 2 ** b for b in range(bits)]
    rows, features = mem_ref.shape
    length = keyin_ref.shape[0]
    head = features // heads
    pairs = heads // 2
    pw = 2 * head
    members = 2 * groups
    g_me = vid * 2 + lax.rem(me, 2)
    scale = head ** (-0.5)

    barrier = pltpu.get_barrier_semaphore()
    for off in range(1, members):
        pl.semaphore_signal(barrier, inc=1, device_id=group_member(groups, lax.rem(g_me + off, members)), device_id_type=MESH)

    for peer in peers:
        pl.semaphore_signal(barrier, inc=1, device_id={"tm": peer * 2 + core}, device_id_type=MESH)

    @pl.when(me > 0)
    def _():
        pl.semaphore_signal(barrier, inc=1, device_id={"tm": me - 1}, device_id_type=MESH)

    @pl.when(me < owners - 1)
    def _():
        pl.semaphore_signal(barrier, inc=1, device_id={"tm": me + 1}, device_id_type=MESH)

    ends = jnp.where(me > 0, 1, 0) + jnp.where(me < owners - 1, 1, 0)
    pl.semaphore_wait(barrier, members - 1 + bits + ends)

    def a_copy(which, src, dst, off):
        g = lax.rem(g_me + off, members)
        return pltpu.make_async_remote_copy(
            src_ref=src, dst_ref=dst.at[g_me], send_sem=a_send.at[which, off], recv_sem=a_recv.at[which, g_me],
            device_id=group_member(groups, g), device_id_type=MESH,
        )

    for off in range(1, members):
        a_copy(0, keyin_ref, a1_ref, off).start()
    a1_ref[g_me] = keyin_ref[...]

    mem = mem_ref[...].astype(F32)
    inv = lax.rsqrt(jnp.mean(mem * mem, axis=-1, keepdims=True) + NORM_EPSILON)
    unit = mem * inv
    unit_ref[...] = unit
    inv_ref[...] = jnp.broadcast_to(inv, inv_ref.shape)
    normed = (unit * gain_ref[...]).astype(BF16)
    mine[1] = normed.astype(F32)
    keyin = keyin_ref[...].astype(BF16)
    qp[...] = dot(normed, wq_ref[...], NN).astype(BF16)
    kp = dot(keyin, wk_ref[...], NN).astype(BF16)
    vp = dot(keyin, wv_ref[...], NN).astype(BF16)
    low = lax.broadcasted_iota(jnp.int32, (length, pw), 1) < head
    zero = jnp.zeros((length, pw), BF16)
    for p in range(pairs):
        kk = kp[:, p * pw:(p + 1) * pw]
        vv = vp[:, p * pw:(p + 1) * pw]
        kbd[p, :length] = jnp.where(low, kk, zero)
        kbd[p, length:] = jnp.where(low, zero, kk)
        vbd[p, :length] = jnp.where(low, vv, zero)
        vbd[p, length:] = jnp.where(low, zero, vv)
    wot[...] = jnp.transpose(wo_ref[...])
    wqt[...] = jnp.transpose(wq_ref[...])
    for p in range(pairs):
        s2 = dot(qp[:, p * pw:(p + 1) * pw], kbd[p], NT)
        for q in range(2):
            h = 2 * p + q
            s = s2[:, q * length:(q + 1) * length] * scale + bias_ref[h:h + 1, :]
            e = jnp.exp(s - jnp.max(s, axis=-1, keepdims=True))
            pr = e / jnp.sum(e, axis=-1, keepdims=True)
            prob[:, h * length:(h + 1) * length] = pr
            half[:, h * length:(h + 1) * length] = pr.astype(BF16)
        mine[0, :, p * pw:(p + 1) * pw] = dot(half[:, p * 2 * length:(p + 1) * 2 * length], vbd[p], NN).astype(BF16).astype(F32)

    for off in range(1, members):
        g = lax.rem(g_me + off, members)
        a_copy(1, mine.at[lax.rem(g, 2)], a2_ref, off).start()
    a2_ref[g_me] = mine[lax.rem(me, 2)]

    live = slot_ref[0].astype(F32)
    step = rows // CHUNKS

    def chain_copy(c):
        return pltpu.make_async_remote_copy(
            src_ref=grad_ref.at[pl.ds(c * step, step)], dst_ref=incoming.at[pl.ds(c * step, step)],
            send_sem=chain_send.at[c], recv_sem=chain_recv.at[c],
            device_id={"tm": jnp.maximum(me - 1, 0)}, device_id_type=MESH,
        )

    @pl.when(me == owners - 1)
    def _():
        incoming[...] = jnp.zeros_like(incoming)

    gain_total = jnp.zeros((1, features), F32)
    for c in range(CHUNKS):
        r = slice(c * step, (c + 1) * step)

        @pl.when(me < owners - 1)
        def _():
            chain_copy(c).wait_recv()

        grad_in = incoming[r, :] + cot_ref[r, :].astype(F32)
        og = (live * grad_in).astype(BF16)
        og_all[r, :] = og
        att = dot(og, wot[...], NN).astype(BF16)
        att_all[r, :] = att
        for p in range(pairs):
            pg2 = dot(att[:, p * pw:(p + 1) * pw], vbd[p], NT)
            for q in range(2):
                h = 2 * p + q
                pg = pg2[:, q * length:(q + 1) * length]
                pr = prob[r, h * length:(h + 1) * length]
                inner = jnp.sum(pr * pg, axis=-1, keepdims=True)
                sg_all[r, h * length:(h + 1) * length] = (pr * (pg - inner) * scale).astype(BF16)
            qg_all[r, p * pw:(p + 1) * pw] = dot(sg_all[r, p * 2 * length:(p + 1) * 2 * length], kbd[p], NN).astype(BF16)
        ng = dot(qg_all[r, :], wqt[...], NN)
        un = unit_ref[r, :]
        gain_total = gain_total + jnp.sum(ng * un, axis=0, keepdims=True)
        sc = ng * gain_ref[...]
        grad_ref[r, :] = grad_in + inv_ref[r, 0:1] * (sc - un * jnp.mean(sc * un, axis=-1, keepdims=True))

        @pl.when(me > 0)
        def _():
            chain_copy(c).start()

    gsum_ref[...] = gain_total

    width = features // groups
    lowr = lax.broadcasted_iota(jnp.int32, (rows, pw), 1) < head
    zr = jnp.zeros((rows, pw), BF16)

    def put(out, which, p, value):
        for v in range(groups):
            lo, hi = max(p * pw, v * width), min((p + 1) * pw, (v + 1) * width)
            if lo < hi:
                out[which, v, :, lo - v * width:hi - v * width] = value[:, lo - p * pw:hi - p * pw]

    for p in range(pairs):
        for which, (left_ref, right_ref) in enumerate(((sg_all, qp), (half, att_all))):
            right = right_ref[:, p * pw:(p + 1) * pw]
            right = jnp.concatenate([jnp.where(lowr, right, zr), jnp.where(lowr, zr, right)], axis=0)
            base = 2 * p * length
            left = jnp.concatenate([left_ref[:, base:base + length], left_ref[:, base + length:base + 2 * length]], axis=0)
            put(b1_ref, which, p, dot(left, right, TN).astype(BF16).astype(F32))
        put(b2_ref, 0, p, og_all[:, p * pw:(p + 1) * pw].astype(F32))
        put(b2_ref, 1, p, qg_all[:, p * pw:(p + 1) * pw].astype(F32))

    def a_arrive():
        for off in range(1, members):
            g = lax.rem(g_me + members - off, members)
            for which, dst in ((0, a1_ref), (1, a2_ref)):
                a_copy(which, dst.at[g_me], dst, off).wait_send()
                pltpu.make_async_remote_copy(
                    src_ref=dst.at[g], dst_ref=dst.at[g], send_sem=a_send.at[which, off], recv_sem=a_recv.at[which, g],
                    device_id=group_member(groups, g), device_id_type=MESH,
                ).wait_recv()

    reduce_part(
        owners, groups, peers, a_arrive, a1_ref, a2_ref, b1_ref, b2_ref, gsum_ref, out_ref, gain_out_ref, *reduce_scratch
    )

    @pl.when(me > 0)
    def _():
        for c in range(CHUNKS):
            chain_copy(c).wait_send()


def reduce_part(
    owners, groups, peers, a_arrive,
    a1_ref, a2_ref, b1_ref, b2_ref, gsum_ref,
    out_ref, gain_ref,
    s1, s2, t1, t2, acc, final, gslot, gacc, gland, *rest,
):
    me = lax.axis_index("tm")
    vid = lax.axis_index("video")
    members = 2 * groups
    chips = owners // 2
    bits = chips.bit_length() - 1
    lands = rest[:bits]
    b_send, b_recv, r_send, r_recv, q_send, q_recv, f_send, f_recv = rest[bits:]
    chip, core = me // 2, lax.rem(me, 2)
    g_me = vid * 2 + core
    pieces, features, pw = acc.shape
    per = pieces // 2
    block = features // chips
    part = block // 2
    scale = 1.0 / (owners * groups)
    length, rows = a1_ref.shape[1], a2_ref.shape[1]

    def b_copy(which, off):
        g = lax.rem(g_me + off, members)
        v, c = lax.div(g, 2), lax.rem(g, 2)
        src, dst = ((b1_ref.at[c, v], s1), (b2_ref.at[c, v], s2), (gsum_ref, gslot))[which]
        return pltpu.make_async_remote_copy(
            src_ref=src, dst_ref=dst.at[g_me], send_sem=b_send.at[which, off], recv_sem=b_recv.at[which, g_me],
            device_id=group_member(groups, g), device_id_type=MESH,
        )

    def b_arrive(which, off):
        g = lax.rem(g_me + members - off, members)
        dst = (s1, s2, gslot)[which]
        return pltpu.make_async_remote_copy(
            src_ref=dst.at[g], dst_ref=dst.at[g], send_sem=b_send.at[which, off], recv_sem=b_recv.at[which, g],
            device_id=group_member(groups, g), device_id_type=MESH,
        )

    for which in (2, 1, 0):
        for off in range(1, members):
            b_copy(which, off).start()
    s1[g_me] = b1_ref[core, vid]
    s2[g_me] = b2_ref[core, vid]
    gslot[g_me] = gsum_ref[...]
    a_arrive()
    for g in range(members):
        t1[:, g * length:(g + 1) * length] = jnp.transpose(a1_ref[g]).astype(BF16)
    for g in range(0, members, 2):
        both = jnp.concatenate([a2_ref[g], a2_ref[g + 1]], axis=0)
        t2[:, g * rows:(g + 2) * rows] = jnp.transpose(both).astype(BF16)

    order = [int(format(i, "b").zfill(bits)[::-1], 2) if bits else 0 for i in range(chips)]

    def products(which):
        slots, left = ((s2, t2), (s1, t1))[which]
        for off in range(1, members):
            b_arrive(1 - which, off).wait_recv()
        for i in range(per):
            right = slots[:, :, i * pw:(i + 1) * pw].reshape(left.shape[1], pw).astype(BF16)
            value = dot(left[...], right, NN)
            for pos in range(chips):
                k = order[pos]
                acc[which * per + i, pos * block:(pos + 1) * block, :] = value[k * block:(k + 1) * block, :]

    starts = []
    lo = 0
    for s in range(bits):
        span = features >> (s + 1)
        bit = lax.rem(lax.div(chip, 2 ** s), 2)
        starts.append((lo + (1 - bit) * span, lo + bit * span, span, peers[s]))
        lo = lo + bit * span

    def r_copy(p, s):
        give, _, span, peer = starts[s]
        return pltpu.make_async_remote_copy(
            src_ref=acc.at[p, pl.ds(pl.multiple_of(give, 8), span)], dst_ref=lands[s].at[p],
            send_sem=r_send.at[p, s], recv_sem=r_recv.at[p, s],
            device_id={"tm": peer * 2 + core}, device_id_type=MESH,
        )

    def g_copy(s):
        return pltpu.make_async_remote_copy(
            src_ref=gacc.at[s], dst_ref=gland.at[s], send_sem=q_send.at[s], recv_sem=q_recv.at[s],
            device_id={"tm": peers[s] * 2 + core}, device_id_type=MESH,
        )

    def r_finish(p, s):
        _, keep, span, _ = starts[s]
        r_copy(p, s).wait_recv()
        at = pl.ds(pl.multiple_of(keep, 8), span)
        acc[p, at, :] = acc[p, at, :] + lands[s][p]

    def f_copy(p):
        theirs = pl.ds(pl.multiple_of(lo + (1 - core) * part, 8), part)
        return pltpu.make_async_remote_copy(
            src_ref=acc.at[p, theirs], dst_ref=final.at[p], send_sem=f_send.at[p], recv_sem=f_recv.at[p],
            device_id={"tm": chip * 2 + 1 - core}, device_id_type=MESH,
        )

    for wave in range(pieces + bits):
        if wave == 0:
            products(0)
        if wave == per:
            products(1)
        for s in reversed(range(bits + 1)):
            p = wave - s
            if 0 <= p < pieces:
                if s > 0:
                    r_finish(p, s - 1)
                if s < bits:
                    r_copy(p, s).start()
                else:
                    f_copy(p).start()
        if wave == 0:
            for off in range(1, members):
                b_arrive(2, off).wait_recv()
            gacc[0] = jnp.sum(gslot[...], axis=0)
        if 0 < wave <= bits:
            g_copy(wave - 1).wait_recv()
            gacc[wave] = gacc[wave - 1] + gland[wave - 1]
        if wave < bits:
            g_copy(wave).start()

    mine_rows = pl.ds(pl.multiple_of(lo + core * part, 8), part)
    for p in range(pieces):
        which, i = p // per, p % per
        cols = slice(i * pw, (i + 1) * pw)
        out_ref[2 * which + core, :, cols] = acc[p, mine_rows, :] * scale
    for p in range(pieces):
        which, i = p // per, p % per
        cols = slice(i * pw, (i + 1) * pw)
        f_copy(p).wait_recv()
        out_ref[2 * which + 1 - core, :, cols] = final[p] * scale

    gain_ref[...] = gacc[bits] * scale
    for s in range(bits):
        g_copy(s).wait_send()
    for which in range(3):
        for off in range(1, members):
            b_copy(which, off).wait_send()
    for p in range(pieces):
        for s in range(bits):
            r_copy(p, s).wait_send()
        f_copy(p).wait_send()


def on_device(
    memory, frames, mem_cot, slot_used, key_bias, start_offset, norm_gain, w_query, w_key, w_value, w_out
):
    owners = lax.axis_size("tm")
    groups = lax.axis_size("video")
    position = lax.axis_index("tm")
    streams, rows, features = memory.shape[2:]
    length = frames.shape[3]
    heads = key_bias.shape[3]
    members = 2 * groups
    chips = owners // 2
    bits = chips.bit_length() - 1
    width = features // groups
    keyin = key_rows(frames[0, 0, 0], start_offset[0, 0], position)
    vmem = pl.BlockSpec(memory_space=pltpu.VMEM)
    smem = pl.BlockSpec(memory_space=pltpu.SMEM)
    sds = jax.ShapeDtypeStruct
    pw = 128 if width % 128 == 0 else width
    pieces = 2 * (width // pw)
    dma = pltpu.SemaphoreType.DMA
    grad, weights, gain = pl.pallas_call(
        functools.partial(whole_kernel, owners, groups, heads),
        out_shape=(
            sds((rows, features), F32),
            sds((4, features // owners, width), F32),
            sds((1, features), F32),
        ),
        in_specs=[smem] + [vmem] * 9,
        out_specs=(vmem,) * 3,
        scratch_shapes=[
            pltpu.VMEM((members, length, features), F32),
            pltpu.VMEM((members, rows, features), F32),
            pltpu.VMEM((2, groups, length, width), F32),
            pltpu.VMEM((2, groups, rows, width), F32),
            pltpu.VMEM((1, features), F32),
            pltpu.VMEM((rows, features), F32),
            pltpu.VMEM((2, rows, features), F32),
            pltpu.VMEM((rows, heads * length), F32),
            pltpu.VMEM((rows, heads * length), BF16),
            pltpu.VMEM((heads // 2, 2 * length, 2 * features // heads), BF16),
            pltpu.VMEM((heads // 2, 2 * length, 2 * features // heads), BF16),
            pltpu.VMEM((rows, features), BF16),
            pltpu.VMEM((rows, features), BF16),
            pltpu.VMEM((rows, heads * length), BF16),
            pltpu.VMEM((rows, features), BF16),
            pltpu.VMEM((rows, features), BF16),
            pltpu.VMEM((rows, features), F32),
            pltpu.VMEM((rows, 128), F32),
            pltpu.VMEM((features, features), BF16),
            pltpu.VMEM((features, features), BF16),
            dma((CHUNKS,)), dma((CHUNKS,)), dma((2, members)), dma((2, members)),
            pltpu.VMEM((members, length, width), F32),
            pltpu.VMEM((members, rows, width), F32),
            pltpu.VMEM((features, members * length), BF16),
            pltpu.VMEM((features, members * rows), BF16),
            pltpu.VMEM((pieces, features, pw), F32),
            pltpu.VMEM((pieces, features // owners, pw), F32),
            pltpu.VMEM((members, 1, features), F32),
            pltpu.VMEM((bits + 1, 1, features), F32),
            pltpu.VMEM((max(bits, 1), 1, features), F32),
        ]
        + [pltpu.VMEM((pieces, features >> (s + 1), pw), F32) for s in range(bits)]
        + [
            dma((3, members)), dma((3, members)), dma((pieces, bits)), dma((pieces, bits)),
            dma((bits,)), dma((bits,)), dma((pieces,)), dma((pieces,)),
        ],
        compiler_params=pltpu.CompilerParams(collective_id=0, has_side_effects=True, vmem_limit_bytes=58 * 1024 * 1024),
        name="whole",
    )(
        slot_used[0, 0], memory[0, 0, 0], keyin, mem_cot[0, 0, 0], key_bias[0, 0, 0],
        norm_gain[None, :], w_query, w_key, w_value, w_out,
    )
    return (grad[None, None, None], weights[1], weights[2], weights[3], weights[0], gain[0])


def solution(mesh):
    return jax.shard_map(
        on_device,
        mesh=mesh,
        in_specs=(
            P("video", "tm", None, None, None),
            P("video", "tm", None, None, None),
            P("video", "tm", None, None, None),
            P("video", "tm", None),
            P("video", "tm", None, None, None),
            P("video", None),
            P(),
            P(),
            P(),
            P(),
            P(),
        ),
        out_specs=(
            P("video", "tm", None, None, None),
            P("tm", "video"),
            P("tm", "video"),
            P("tm", "video"),
            P("tm", "video"),
            P(),
        ),
        check_vma=False,
    )
```

```python
import functools
import math

import jax
import jax.numpy as jnp
from jax import lax
from jax.experimental import pallas as pl
from jax.experimental.pallas import tpu as pltpu
from jax.sharding import PartitionSpec as P

NORM_EPSILON = 1e-06
MESH = pl.DeviceIdType.MESH
F32 = jnp.float32
BF16 = jnp.bfloat16
NN = (((1,), (0,)), ((), ()))
NT = (((1,), (1,)), ((), ()))
TN = (((0,), (0,)), ((), ()))
CHUNKS = 4


def dot(left, right, form):
    return lax.dot_general(left, right, form, preferred_element_type=F32)


def key_rows(frame_rows, offset, position):
    length, features = frame_rows.shape
    within = jnp.arange(length, dtype=jnp.int32)
    frame_time = (offset + position * length + within).astype(F32)
    half_width = features // 2
    frequency = 0.0625 * jnp.exp(-math.log(1000.0) * jnp.arange(half_width, dtype=F32) / half_width)
    phases = frame_time[:, None] * frequency
    return frame_rows + jnp.concatenate([jnp.sin(phases), jnp.cos(phases)], axis=-1)


def group_member(groups, g):
    me = lax.axis_index("tm")
    return {"video": lax.div(g, 2), "tm": (me // 2) * 2 + lax.rem(g, 2)}


def whole_kernel(
    owners, groups, heads,
    slot_ref, mem_ref, keyin_ref, cot_ref, bias_ref, gain_ref, wq_ref, wk_ref, wv_ref, wo_ref,
    grad_ref, out_ref, gain_out_ref,
    a1_ref, a2_ref, b1_ref, b2_ref, gsum_ref,
    incoming, mine, prob, half, kbd, vbd, qp, att_all, sg_all, og_all, qg_all, unit_ref, inv_ref, wot, wqt,
    chain_send, chain_recv, a_send, a_recv,
    *reduce_scratch,
):
    me = lax.axis_index("tm")
    vid = lax.axis_index("video")
    chips = owners // 2
    bits = chips.bit_length() - 1
    chip, core = me // 2, lax.rem(me, 2)
    peers = [chip + (1 - 2 * lax.rem(lax.div(chip, 2 ** b), 2)) * 2 ** b for b in range(bits)]
    rows, features = mem_ref.shape
    length = keyin_ref.shape[0]
    head = features // heads
    pairs = heads // 2
    pw = 2 * head
    members = 2 * groups
    g_me = vid * 2 + lax.rem(me, 2)
    scale = head ** (-0.5)

    barrier = pltpu.get_barrier_semaphore()
    for off in range(1, members):
        pl.semaphore_signal(barrier, inc=1, device_id=group_member(groups, lax.rem(g_me + off, members)), device_id_type=MESH)

    for peer in peers:
        pl.semaphore_signal(barrier, inc=1, device_id={"tm": peer * 2 + core}, device_id_type=MESH)

    @pl.when(me > 0)
    def _():
        pl.semaphore_signal(barrier, inc=1, device_id={"tm": me - 1}, device_id_type=MESH)

    @pl.when(me < owners - 1)
    def _():
        pl.semaphore_signal(barrier, inc=1, device_id={"tm": me + 1}, device_id_type=MESH)

    ends = jnp.where(me > 0, 1, 0) + jnp.where(me < owners - 1, 1, 0)
    pl.semaphore_wait(barrier, members - 1 + bits + ends)

    def a_copy(which, src, dst, off):
        g = lax.rem(g_me + off, members)
        return pltpu.make_async_remote_copy(
            src_ref=src, dst_ref=dst.at[g_me], send_sem=a_send.at[which, off], recv_sem=a_recv.at[which, g_me],
            device_id=group_member(groups, g), device_id_type=MESH,
        )

    for off in range(1, members):
        a_copy(0, keyin_ref, a1_ref, off).start()
    a1_ref[g_me] = keyin_ref[...]

    mem = mem_ref[...].astype(F32)
    inv = lax.rsqrt(jnp.mean(mem * mem, axis=-1, keepdims=True) + NORM_EPSILON)
    unit = mem * inv
    unit_ref[...] = unit
    inv_ref[...] = jnp.broadcast_to(inv, inv_ref.shape)
    normed = (unit * gain_ref[...]).astype(BF16)
    mine[1] = normed.astype(F32)
    keyin = keyin_ref[...].astype(BF16)
    query = dot(normed, wq_ref[...], NN).astype(BF16)
    qp[...] = query
    kp = dot(keyin, wk_ref[...], NN).astype(BF16)
    vp = dot(keyin, wv_ref[...], NN).astype(BF16)
    low = lax.broadcasted_iota(jnp.int32, (length, pw), 1) < head
    zero = jnp.zeros((length, pw), BF16)
    for p in range(pairs):
        kk = kp[:, p * pw:(p + 1) * pw]
        vv = vp[:, p * pw:(p + 1) * pw]
        kbd[p, :length] = jnp.where(low, kk, zero)
        kbd[p, length:] = jnp.where(low, zero, kk)
        vbd[p, :length] = jnp.where(low, vv, zero)
        vbd[p, length:] = jnp.where(low, zero, vv)
    wot[...] = jnp.transpose(wo_ref[...])
    wqt[...] = jnp.transpose(wq_ref[...])
    scores = [dot(query[:, p * pw:(p + 1) * pw], kbd[p], NT) for p in range(pairs)]
    for p in range(pairs):
        halves = []
        for q in range(2):
            h = 2 * p + q
            s = scores[p][:, q * length:(q + 1) * length] * scale + bias_ref[h:h + 1, :]
            e = jnp.exp(s - jnp.max(s, axis=-1, keepdims=True))
            pr = e / jnp.sum(e, axis=-1, keepdims=True)
            prob[:, h * length:(h + 1) * length] = pr
            halves.append(pr.astype(BF16))
        both = jnp.concatenate(halves, axis=-1)
        half[:, p * 2 * length:(p + 1) * 2 * length] = both
        mine[0, :, p * pw:(p + 1) * pw] = dot(both, vbd[p], NN).astype(BF16).astype(F32)

    for off in range(1, members):
        g = lax.rem(g_me + off, members)
        a_copy(1, mine.at[lax.rem(g, 2)], a2_ref, off).start()
    a2_ref[g_me] = mine[lax.rem(me, 2)]

    live = slot_ref[0].astype(F32)
    step = rows // CHUNKS

    def chain_copy(c):
        return pltpu.make_async_remote_copy(
            src_ref=grad_ref.at[pl.ds(c * step, step)], dst_ref=incoming.at[pl.ds(c * step, step)],
            send_sem=chain_send.at[c], recv_sem=chain_recv.at[c],
            device_id={"tm": jnp.maximum(me - 1, 0)}, device_id_type=MESH,
        )

    @pl.when(me == owners - 1)
    def _():
        incoming[...] = jnp.zeros_like(incoming)

    gain_total = jnp.zeros((1, features), F32)
    for c in range(CHUNKS):
        r = slice(c * step, (c + 1) * step)

        @pl.when(me < owners - 1)
        def _():
            chain_copy(c).wait_recv()

        grad_in = incoming[r, :] + cot_ref[r, :].astype(F32)
        og = (live * grad_in).astype(BF16)
        att = dot(og, wot[...], NN).astype(BF16)
        prob_grads = [dot(att[:, p * pw:(p + 1) * pw], vbd[p], NT) for p in range(pairs)]
        query_grads = []
        score_grads = []
        for p in range(pairs):
            for q in range(2):
                h = 2 * p + q
                pg = prob_grads[p][:, q * length:(q + 1) * length]
                pr = prob[r, h * length:(h + 1) * length]
                inner = jnp.sum(pr * pg, axis=-1, keepdims=True)
                score_grads.append((pr * (pg - inner) * scale).astype(BF16))
            query_grads.append(dot(jnp.concatenate(score_grads[-2:], axis=-1), kbd[p], NN).astype(BF16))
        qg = jnp.concatenate(query_grads, axis=-1)
        ng = dot(qg, wqt[...], NN)
        un = unit_ref[r, :]
        gain_total = gain_total + jnp.sum(ng * un, axis=0, keepdims=True)
        sc = ng * gain_ref[...]
        grad_ref[r, :] = grad_in + inv_ref[r, 0:1] * (sc - un * jnp.mean(sc * un, axis=-1, keepdims=True))

        @pl.when(me > 0)
        def _():
            chain_copy(c).start()

        og_all[r, :] = og
        att_all[r, :] = att
        qg_all[r, :] = qg
        for h in range(heads):
            sg_all[r, h * length:(h + 1) * length] = score_grads[h]

    gsum_ref[...] = gain_total

    width = features // groups
    lowr = lax.broadcasted_iota(jnp.int32, (rows, pw), 1) < head
    zr = jnp.zeros((rows, pw), BF16)

    def put(out, which, p, value):
        for v in range(groups):
            lo, hi = max(p * pw, v * width), min((p + 1) * pw, (v + 1) * width)
            if lo < hi:
                out[which, v, :, lo - v * width:hi - v * width] = value[:, lo - p * pw:hi - p * pw]

    for p in range(pairs):
        for which, (left_ref, right_ref) in enumerate(((sg_all, qp), (half, att_all))):
            right = right_ref[:, p * pw:(p + 1) * pw]
            right = jnp.concatenate([jnp.where(lowr, right, zr), jnp.where(lowr, zr, right)], axis=0)
            base = 2 * p * length
            left = jnp.concatenate([left_ref[:, base:base + length], left_ref[:, base + length:base + 2 * length]], axis=0)
            put(b1_ref, which, p, dot(left, right, TN).astype(BF16).astype(F32))
        put(b2_ref, 0, p, og_all[:, p * pw:(p + 1) * pw].astype(F32))
        put(b2_ref, 1, p, qg_all[:, p * pw:(p + 1) * pw].astype(F32))

    def a_arrive():
        for off in range(1, members):
            g = lax.rem(g_me + members - off, members)
            for which, dst in ((0, a1_ref), (1, a2_ref)):
                a_copy(which, dst.at[g_me], dst, off).wait_send()
                pltpu.make_async_remote_copy(
                    src_ref=dst.at[g], dst_ref=dst.at[g], send_sem=a_send.at[which, off], recv_sem=a_recv.at[which, g],
                    device_id=group_member(groups, g), device_id_type=MESH,
                ).wait_recv()

    reduce_part(
        owners, groups, peers, a_arrive, a1_ref, a2_ref, b1_ref, b2_ref, gsum_ref, out_ref, gain_out_ref, *reduce_scratch
    )

    @pl.when(me > 0)
    def _():
        for c in range(CHUNKS):
            chain_copy(c).wait_send()


def reduce_part(
    owners, groups, peers, a_arrive,
    a1_ref, a2_ref, b1_ref, b2_ref, gsum_ref,
    out_ref, gain_ref,
    s1, s2, t1, t2, acc, final, gslot, gacc, gland, *rest,
):
    me = lax.axis_index("tm")
    vid = lax.axis_index("video")
    members = 2 * groups
    chips = owners // 2
    bits = chips.bit_length() - 1
    lands = rest[:bits]
    b_send, b_recv, r_send, r_recv, q_send, q_recv, f_send, f_recv = rest[bits:]
    chip, core = me // 2, lax.rem(me, 2)
    g_me = vid * 2 + core
    pieces, features, pw = acc.shape
    per = pieces // 2
    block = features // chips
    part = block // 2
    scale = 1.0 / (owners * groups)
    length, rows = a1_ref.shape[1], a2_ref.shape[1]

    def b_copy(which, off):
        g = lax.rem(g_me + off, members)
        v, c = lax.div(g, 2), lax.rem(g, 2)
        src, dst = ((b1_ref.at[c, v], s1), (b2_ref.at[c, v], s2), (gsum_ref, gslot))[which]
        return pltpu.make_async_remote_copy(
            src_ref=src, dst_ref=dst.at[g_me], send_sem=b_send.at[which, off], recv_sem=b_recv.at[which, g_me],
            device_id=group_member(groups, g), device_id_type=MESH,
        )

    def b_arrive(which, off):
        g = lax.rem(g_me + members - off, members)
        dst = (s1, s2, gslot)[which]
        return pltpu.make_async_remote_copy(
            src_ref=dst.at[g], dst_ref=dst.at[g], send_sem=b_send.at[which, off], recv_sem=b_recv.at[which, g],
            device_id=group_member(groups, g), device_id_type=MESH,
        )

    for which in (2, 1, 0):
        for off in range(1, members):
            b_copy(which, off).start()
    s1[g_me] = b1_ref[core, vid]
    s2[g_me] = b2_ref[core, vid]
    gslot[g_me] = gsum_ref[...]
    a_arrive()
    for g in range(members):
        t1[:, g * length:(g + 1) * length] = jnp.transpose(a1_ref[g]).astype(BF16)
    for g in range(0, members, 2):
        both = jnp.concatenate([a2_ref[g], a2_ref[g + 1]], axis=0)
        t2[:, g * rows:(g + 2) * rows] = jnp.transpose(both).astype(BF16)

    order = [int(format(i, "b").zfill(bits)[::-1], 2) if bits else 0 for i in range(chips)]

    def products(which):
        slots, left = ((s2, t2), (s1, t1))[which]
        for off in range(1, members):
            b_arrive(1 - which, off).wait_recv()
        for i in range(per):
            right = slots[:, :, i * pw:(i + 1) * pw].reshape(left.shape[1], pw).astype(BF16)
            value = dot(left[...], right, NN)
            for pos in range(chips):
                k = order[pos]
                acc[which * per + i, pos * block:(pos + 1) * block, :] = value[k * block:(k + 1) * block, :]

    starts = []
    lo = 0
    for s in range(bits):
        span = features >> (s + 1)
        bit = lax.rem(lax.div(chip, 2 ** s), 2)
        starts.append((lo + (1 - bit) * span, lo + bit * span, span, peers[s]))
        lo = lo + bit * span

    def r_copy(p, s):
        give, _, span, peer = starts[s]
        return pltpu.make_async_remote_copy(
            src_ref=acc.at[p, pl.ds(pl.multiple_of(give, 8), span)], dst_ref=lands[s].at[p],
            send_sem=r_send.at[p, s], recv_sem=r_recv.at[p, s],
            device_id={"tm": peer * 2 + core}, device_id_type=MESH,
        )

    def g_copy(s):
        return pltpu.make_async_remote_copy(
            src_ref=gacc.at[s], dst_ref=gland.at[s], send_sem=q_send.at[s], recv_sem=q_recv.at[s],
            device_id={"tm": peers[s] * 2 + core}, device_id_type=MESH,
        )

    def r_finish(p, s):
        _, keep, span, _ = starts[s]
        r_copy(p, s).wait_recv()
        at = pl.ds(pl.multiple_of(keep, 8), span)
        acc[p, at, :] = acc[p, at, :] + lands[s][p]

    def f_copy(p):
        theirs = pl.ds(pl.multiple_of(lo + (1 - core) * part, 8), part)
        return pltpu.make_async_remote_copy(
            src_ref=acc.at[p, theirs], dst_ref=final.at[p], send_sem=f_send.at[p], recv_sem=f_recv.at[p],
            device_id={"tm": chip * 2 + 1 - core}, device_id_type=MESH,
        )

    for wave in range(pieces + bits):
        if wave == 0:
            products(0)
        if wave == per:
            products(1)
        for s in reversed(range(bits + 1)):
            p = wave - s
            if 0 <= p < pieces:
                if s > 0:
                    r_finish(p, s - 1)
                if s < bits:
                    r_copy(p, s).start()
                else:
                    f_copy(p).start()
        if wave == 0:
            for off in range(1, members):
                b_arrive(2, off).wait_recv()
            gacc[0] = jnp.sum(gslot[...], axis=0)
        if 0 < wave <= bits:
            g_copy(wave - 1).wait_recv()
            gacc[wave] = gacc[wave - 1] + gland[wave - 1]
        if wave < bits:
            g_copy(wave).start()

    mine_rows = pl.ds(pl.multiple_of(lo + core * part, 8), part)
    for p in range(pieces):
        which, i = p // per, p % per
        cols = slice(i * pw, (i + 1) * pw)
        out_ref[2 * which + core, :, cols] = acc[p, mine_rows, :] * scale
    for p in range(pieces):
        which, i = p // per, p % per
        cols = slice(i * pw, (i + 1) * pw)
        f_copy(p).wait_recv()
        out_ref[2 * which + 1 - core, :, cols] = final[p] * scale

    gain_ref[...] = gacc[bits] * scale
    for s in range(bits):
        g_copy(s).wait_send()
    for which in range(3):
        for off in range(1, members):
            b_copy(which, off).wait_send()
    for p in range(pieces):
        for s in range(bits):
            r_copy(p, s).wait_send()
        f_copy(p).wait_send()


def on_device(
    memory, frames, mem_cot, slot_used, key_bias, start_offset, norm_gain, w_query, w_key, w_value, w_out
):
    owners = lax.axis_size("tm")
    groups = lax.axis_size("video")
    position = lax.axis_index("tm")
    streams, rows, features = memory.shape[2:]
    length = frames.shape[3]
    heads = key_bias.shape[3]
    members = 2 * groups
    chips = owners // 2
    bits = chips.bit_length() - 1
    width = features // groups
    keyin = key_rows(frames[0, 0, 0], start_offset[0, 0], position)
    vmem = pl.BlockSpec(memory_space=pltpu.VMEM)
    smem = pl.BlockSpec(memory_space=pltpu.SMEM)
    sds = jax.ShapeDtypeStruct
    pw = 128 if width % 128 == 0 else width
    pieces = 2 * (width // pw)
    dma = pltpu.SemaphoreType.DMA
    grad, weights, gain = pl.pallas_call(
        functools.partial(whole_kernel, owners, groups, heads),
        out_shape=(
            sds((rows, features), F32),
            sds((4, features // owners, width), F32),
            sds((1, features), F32),
        ),
        in_specs=[smem] + [vmem] * 9,
        out_specs=(vmem,) * 3,
        scratch_shapes=[
            pltpu.VMEM((members, length, features), F32),
            pltpu.VMEM((members, rows, features), F32),
            pltpu.VMEM((2, groups, length, width), F32),
            pltpu.VMEM((2, groups, rows, width), F32),
            pltpu.VMEM((1, features), F32),
            pltpu.VMEM((rows, features), F32),
            pltpu.VMEM((2, rows, features), F32),
            pltpu.VMEM((rows, heads * length), F32),
            pltpu.VMEM((rows, heads * length), BF16),
            pltpu.VMEM((heads // 2, 2 * length, 2 * features // heads), BF16),
            pltpu.VMEM((heads // 2, 2 * length, 2 * features // heads), BF16),
            pltpu.VMEM((rows, features), BF16),
            pltpu.VMEM((rows, features), BF16),
            pltpu.VMEM((rows, heads * length), BF16),
            pltpu.VMEM((rows, features), BF16),
            pltpu.VMEM((rows, features), BF16),
            pltpu.VMEM((rows, features), F32),
            pltpu.VMEM((rows, 128), F32),
            pltpu.VMEM((features, features), BF16),
            pltpu.VMEM((features, features), BF16),
            dma((CHUNKS,)), dma((CHUNKS,)), dma((2, members)), dma((2, members)),
            pltpu.VMEM((members, length, width), F32),
            pltpu.VMEM((members, rows, width), F32),
            pltpu.VMEM((features, members * length), BF16),
            pltpu.VMEM((features, members * rows), BF16),
            pltpu.VMEM((pieces, features, pw), F32),
            pltpu.VMEM((pieces, features // owners, pw), F32),
            pltpu.VMEM((members, 1, features), F32),
            pltpu.VMEM((bits + 1, 1, features), F32),
            pltpu.VMEM((max(bits, 1), 1, features), F32),
        ]
        + [pltpu.VMEM((pieces, features >> (s + 1), pw), F32) for s in range(bits)]
        + [
            dma((3, members)), dma((3, members)), dma((pieces, bits)), dma((pieces, bits)),
            dma((bits,)), dma((bits,)), dma((pieces,)), dma((pieces,)),
        ],
        compiler_params=pltpu.CompilerParams(collective_id=0, has_side_effects=True, vmem_limit_bytes=58 * 1024 * 1024),
        name="whole",
    )(
        slot_used[0, 0], memory[0, 0, 0], keyin, mem_cot[0, 0, 0], key_bias[0, 0, 0],
        norm_gain[None, :], w_query, w_key, w_value, w_out,
    )
    return (grad[None, None, None], weights[1], weights[2], weights[3], weights[0], gain[0])


def solution(mesh):
    return jax.shard_map(
        on_device,
        mesh=mesh,
        in_specs=(
            P("video", "tm", None, None, None),
            P("video", "tm", None, None, None),
            P("video", "tm", None, None, None),
            P("video", "tm", None),
            P("video", "tm", None, None, None),
            P("video", None),
            P(),
            P(),
            P(),
            P(),
            P(),
        ),
        out_specs=(
            P("video", "tm", None, None, None),
            P("tm", "video"),
            P("tm", "video"),
            P("tm", "video"),
            P("tm", "video"),
            P(),
        ),
        check_vma=False,
    )
```

```python
import functools
import math

import jax
import jax.numpy as jnp
from jax import lax
from jax.experimental import pallas as pl
from jax.experimental.pallas import tpu as pltpu
from jax.sharding import PartitionSpec as P

NORM_EPSILON = 1e-06
MESH = pl.DeviceIdType.MESH
F32 = jnp.float32
BF16 = jnp.bfloat16
NN = (((1,), (0,)), ((), ()))
NT = (((1,), (1,)), ((), ()))
TN = (((0,), (0,)), ((), ()))
CHUNKS = 4


def dot(left, right, form):
    return lax.dot_general(left, right, form, preferred_element_type=F32)


def key_rows(frame_rows, offset, position):
    length, features = frame_rows.shape
    within = jnp.arange(length, dtype=jnp.int32)
    frame_time = (offset + position * length + within).astype(F32)
    half_width = features // 2
    frequency = 0.0625 * jnp.exp(-math.log(1000.0) * jnp.arange(half_width, dtype=F32) / half_width)
    phases = frame_time[:, None] * frequency
    return frame_rows + jnp.concatenate([jnp.sin(phases), jnp.cos(phases)], axis=-1)


def group_member(groups, g):
    me = lax.axis_index("tm")
    return {"video": lax.div(g, 2), "tm": (me // 2) * 2 + lax.rem(g, 2)}


def whole_kernel(
    owners, groups, heads,
    slot_ref, mem_ref, keyin_ref, cot_ref, bias_ref, gain_ref, wq_ref, wk_ref, wv_ref, wo_ref,
    grad_ref, out_ref, gain_out_ref,
    a1_ref, a2_ref, b1_ref, b2_ref, gsum_ref,
    incoming, mine, prob, half, kbd, vbd, qp, att_all, sg_all, og_all, qg_all, unit_ref, inv_ref, wot, wqt,
    chain_send, chain_recv, a_send, a_recv,
    *reduce_scratch,
):
    me = lax.axis_index("tm")
    vid = lax.axis_index("video")
    chips = owners // 2
    bits = chips.bit_length() - 1
    chip, core = me // 2, lax.rem(me, 2)
    peers = [chip + (1 - 2 * lax.rem(lax.div(chip, 2 ** b), 2)) * 2 ** b for b in range(bits)]
    rows, features = mem_ref.shape
    length = keyin_ref.shape[0]
    head = features // heads
    pairs = heads // 2
    pw = 2 * head
    members = 2 * groups
    g_me = vid * 2 + lax.rem(me, 2)
    scale = head ** (-0.5)

    barrier = pltpu.get_barrier_semaphore()
    for off in range(1, members):
        pl.semaphore_signal(barrier, inc=1, device_id=group_member(groups, lax.rem(g_me + off, members)), device_id_type=MESH)

    for peer in peers:
        pl.semaphore_signal(barrier, inc=1, device_id={"tm": peer * 2 + core}, device_id_type=MESH)

    @pl.when(me > 0)
    def _():
        pl.semaphore_signal(barrier, inc=1, device_id={"tm": me - 1}, device_id_type=MESH)

    @pl.when(me < owners - 1)
    def _():
        pl.semaphore_signal(barrier, inc=1, device_id={"tm": me + 1}, device_id_type=MESH)

    ends = jnp.where(me > 0, 1, 0) + jnp.where(me < owners - 1, 1, 0)
    pl.semaphore_wait(barrier, members - 1 + bits + ends)

    def a_copy(which, src, dst, off):
        g = lax.rem(g_me + off, members)
        return pltpu.make_async_remote_copy(
            src_ref=src, dst_ref=dst.at[g_me], send_sem=a_send.at[which, off], recv_sem=a_recv.at[which, g_me],
            device_id=group_member(groups, g), device_id_type=MESH,
        )

    for off in range(1, members):
        a_copy(0, keyin_ref, a1_ref, off).start()
    a1_ref[g_me] = keyin_ref[...]

    mem = mem_ref[...].astype(F32)
    inv = lax.rsqrt(jnp.mean(mem * mem, axis=-1, keepdims=True) + NORM_EPSILON)
    unit = mem * inv
    unit_ref[...] = unit
    inv_ref[...] = jnp.broadcast_to(inv, inv_ref.shape)
    normed = (unit * gain_ref[...]).astype(BF16)
    mine[1] = normed.astype(F32)
    keyin = keyin_ref[...].astype(BF16)
    query = dot(normed, wq_ref[...], NN).astype(BF16)
    qp[...] = query
    kp = dot(keyin, wk_ref[...], NN).astype(BF16)
    vp = dot(keyin, wv_ref[...], NN).astype(BF16)
    low = lax.broadcasted_iota(jnp.int32, (length, pw), 1) < head
    zero = jnp.zeros((length, pw), BF16)
    for p in range(pairs):
        kk = kp[:, p * pw:(p + 1) * pw]
        vv = vp[:, p * pw:(p + 1) * pw]
        kbd[p, :length] = jnp.where(low, kk, zero)
        kbd[p, length:] = jnp.where(low, zero, kk)
        vbd[p, :length] = jnp.where(low, vv, zero)
        vbd[p, length:] = jnp.where(low, zero, vv)
    wot[...] = jnp.transpose(wo_ref[...])
    wqt[...] = jnp.transpose(wq_ref[...])
    scores = [dot(query[:, p * pw:(p + 1) * pw], kbd[p], NT) for p in range(pairs)]
    for p in range(pairs):
        halves = []
        for q in range(2):
            h = 2 * p + q
            s = scores[p][:, q * length:(q + 1) * length] * scale + bias_ref[h:h + 1, :]
            e = jnp.exp(s - jnp.max(s, axis=-1, keepdims=True))
            pr = e / jnp.sum(e, axis=-1, keepdims=True)
            prob[:, h * length:(h + 1) * length] = pr
            halves.append(pr.astype(BF16))
        both = jnp.concatenate(halves, axis=-1)
        half[:, p * 2 * length:(p + 1) * 2 * length] = both
        mine[0, :, p * pw:(p + 1) * pw] = dot(both, vbd[p], NN).astype(BF16).astype(F32)

    for off in range(1, members):
        g = lax.rem(g_me + off, members)
        a_copy(1, mine.at[lax.rem(g, 2)], a2_ref, off).start()
    a2_ref[g_me] = mine[lax.rem(me, 2)]

    def a_arrive():
        for off in range(1, members):
            g = lax.rem(g_me + members - off, members)
            for which, dst in ((0, a1_ref), (1, a2_ref)):
                a_copy(which, dst.at[g_me], dst, off).wait_send()
                pltpu.make_async_remote_copy(
                    src_ref=dst.at[g], dst_ref=dst.at[g], send_sem=a_send.at[which, off], recv_sem=a_recv.at[which, g],
                    device_id=group_member(groups, g), device_id_type=MESH,
                ).wait_recv()
        t1, t2 = reduce_scratch[2:4]
        for g in range(members):
            t1[:, g * length:(g + 1) * length] = jnp.transpose(a1_ref[g]).astype(BF16)
        for g in range(0, members, 2):
            both = jnp.concatenate([a2_ref[g], a2_ref[g + 1]], axis=0)
            t2[:, g * rows:(g + 2) * rows] = jnp.transpose(both).astype(BF16)

    @pl.when(me < owners // 4)
    def _():
        a_arrive()

    live = slot_ref[0].astype(F32)
    step = rows // CHUNKS

    def chain_copy(c):
        return pltpu.make_async_remote_copy(
            src_ref=grad_ref.at[pl.ds(c * step, step)], dst_ref=incoming.at[pl.ds(c * step, step)],
            send_sem=chain_send.at[c], recv_sem=chain_recv.at[c],
            device_id={"tm": jnp.maximum(me - 1, 0)}, device_id_type=MESH,
        )

    @pl.when(me == owners - 1)
    def _():
        incoming[...] = jnp.zeros_like(incoming)

    gain_total = jnp.zeros((1, features), F32)
    for c in range(CHUNKS):
        r = slice(c * step, (c + 1) * step)

        @pl.when(me < owners - 1)
        def _():
            chain_copy(c).wait_recv()

        grad_in = incoming[r, :] + cot_ref[r, :].astype(F32)
        og = (live * grad_in).astype(BF16)
        att = dot(og, wot[...], NN).astype(BF16)
        prob_grads = [dot(att[:, p * pw:(p + 1) * pw], vbd[p], NT) for p in range(pairs)]
        query_grads = []
        score_grads = []
        for p in range(pairs):
            for q in range(2):
                h = 2 * p + q
                pg = prob_grads[p][:, q * length:(q + 1) * length]
                pr = prob[r, h * length:(h + 1) * length]
                inner = jnp.sum(pr * pg, axis=-1, keepdims=True)
                score_grads.append((pr * (pg - inner) * scale).astype(BF16))
            query_grads.append(dot(jnp.concatenate(score_grads[-2:], axis=-1), kbd[p], NN).astype(BF16))
        qg = jnp.concatenate(query_grads, axis=-1)
        ng = dot(qg, wqt[...], NN)
        un = unit_ref[r, :]
        gain_total = gain_total + jnp.sum(ng * un, axis=0, keepdims=True)
        sc = ng * gain_ref[...]
        grad_ref[r, :] = grad_in + inv_ref[r, 0:1] * (sc - un * jnp.mean(sc * un, axis=-1, keepdims=True))

        @pl.when(me > 0)
        def _():
            chain_copy(c).start()

        og_all[r, :] = og
        att_all[r, :] = att
        qg_all[r, :] = qg
        for h in range(heads):
            sg_all[r, h * length:(h + 1) * length] = score_grads[h]

    gsum_ref[...] = gain_total

    width = features // groups
    lowr = lax.broadcasted_iota(jnp.int32, (rows, pw), 1) < head
    zr = jnp.zeros((rows, pw), BF16)

    def put(out, which, p, value):
        for v in range(groups):
            lo, hi = max(p * pw, v * width), min((p + 1) * pw, (v + 1) * width)
            if lo < hi:
                out[which, v, :, lo - v * width:hi - v * width] = value[:, lo - p * pw:hi - p * pw]

    for p in range(pairs):
        put(b2_ref, 0, p, og_all[:, p * pw:(p + 1) * pw].astype(F32))
        put(b2_ref, 1, p, qg_all[:, p * pw:(p + 1) * pw].astype(F32))

    def token_grads():
        for p in range(pairs):
            for which, (left_ref, right_ref) in enumerate(((sg_all, qp), (half, att_all))):
                right = right_ref[:, p * pw:(p + 1) * pw]
                right = jnp.concatenate([jnp.where(lowr, right, zr), jnp.where(lowr, zr, right)], axis=0)
                base = 2 * p * length
                left = jnp.concatenate([left_ref[:, base:base + length], left_ref[:, base + length:base + 2 * length]], axis=0)
                put(b1_ref, which, p, dot(left, right, TN).astype(BF16).astype(F32))

    reduce_part(
        owners, groups, peers, token_grads, a_arrive, b1_ref, b2_ref, gsum_ref, out_ref, gain_out_ref, *reduce_scratch
    )

    @pl.when(me > 0)
    def _():
        for c in range(CHUNKS):
            chain_copy(c).wait_send()


def reduce_part(
    owners, groups, peers, token_grads, a_arrive,
    b1_ref, b2_ref, gsum_ref,
    out_ref, gain_ref,
    s1, s2, t1, t2, acc, final, gslot, gacc, gland, *rest,
):
    me = lax.axis_index("tm")
    vid = lax.axis_index("video")
    members = 2 * groups
    chips = owners // 2
    bits = chips.bit_length() - 1
    lands = rest[:bits]
    b_send, b_recv, r_send, r_recv, q_send, q_recv, f_send, f_recv = rest[bits:]
    chip, core = me // 2, lax.rem(me, 2)
    g_me = vid * 2 + core
    pieces, features, pw = acc.shape
    per = pieces // 2
    block = features // chips
    part = block // 2
    scale = 1.0 / (owners * groups)

    def b_copy(which, off):
        g = lax.rem(g_me + off, members)
        v, c = lax.div(g, 2), lax.rem(g, 2)
        src, dst = ((b1_ref.at[c, v], s1), (b2_ref.at[c, v], s2), (gsum_ref, gslot))[which]
        return pltpu.make_async_remote_copy(
            src_ref=src, dst_ref=dst.at[g_me], send_sem=b_send.at[which, off], recv_sem=b_recv.at[which, g_me],
            device_id=group_member(groups, g), device_id_type=MESH,
        )

    def b_arrive(which, off):
        g = lax.rem(g_me + members - off, members)
        dst = (s1, s2, gslot)[which]
        return pltpu.make_async_remote_copy(
            src_ref=dst.at[g], dst_ref=dst.at[g], send_sem=b_send.at[which, off], recv_sem=b_recv.at[which, g],
            device_id=group_member(groups, g), device_id_type=MESH,
        )

    for which in (2, 1):
        for off in range(1, members):
            b_copy(which, off).start()
    token_grads()
    for off in range(1, members):
        b_copy(0, off).start()
    s1[g_me] = b1_ref[core, vid]
    s2[g_me] = b2_ref[core, vid]
    gslot[g_me] = gsum_ref[...]

    @pl.when(me >= owners // 4)
    def _():
        a_arrive()

    plain = list(range(bits))
    swapped = plain[1::-1] + plain[2:]
    sequence = [swapped if per > 1 and bits > 1 and p % per == 0 else plain for p in range(pieces)]

    def products(which):
        slots, left = ((s2, t2), (s1, t1))[which]
        for off in range(1, members):
            b_arrive(1 - which, off).wait_recv()
        for i in range(per):
            right = slots[:, :, i * pw:(i + 1) * pw].reshape(left.shape[1], pw).astype(BF16)
            value = dot(left[...], right, NN)
            for pos in range(chips):
                k = sum(((pos >> (bits - 1 - n)) & 1) << bit for n, bit in enumerate(sequence[which * per + i]))
                acc[which * per + i, pos * block:(pos + 1) * block, :] = value[k * block:(k + 1) * block, :]

    starts, home = [], []
    for p in range(pieces):
        stages, lo = [], 0
        for n, b in enumerate(sequence[p]):
            span = features >> (n + 1)
            bit = lax.rem(lax.div(chip, 2 ** b), 2)
            stages.append((lo + (1 - bit) * span, lo + bit * span, span, peers[b]))
            lo = lo + bit * span
        starts.append(stages)
        home.append(lo)

    def r_copy(p, s):
        give, _, span, peer = starts[p][s]
        return pltpu.make_async_remote_copy(
            src_ref=acc.at[p, pl.ds(pl.multiple_of(give, 8), span)], dst_ref=lands[s].at[p],
            send_sem=r_send.at[p, s], recv_sem=r_recv.at[p, s],
            device_id={"tm": peer * 2 + core}, device_id_type=MESH,
        )

    def g_copy(s):
        return pltpu.make_async_remote_copy(
            src_ref=gacc.at[s], dst_ref=gland.at[s], send_sem=q_send.at[s], recv_sem=q_recv.at[s],
            device_id={"tm": peers[s] * 2 + core}, device_id_type=MESH,
        )

    def r_finish(p, s):
        _, keep, span, _ = starts[p][s]
        r_copy(p, s).wait_recv()
        at = pl.ds(pl.multiple_of(keep, 8), span)
        acc[p, at, :] = acc[p, at, :] + lands[s][p]

    def f_copy(p):
        theirs = pl.ds(pl.multiple_of(home[p] + (1 - core) * part, 8), part)
        return pltpu.make_async_remote_copy(
            src_ref=acc.at[p, theirs], dst_ref=final.at[p], send_sem=f_send.at[p], recv_sem=f_recv.at[p],
            device_id={"tm": chip * 2 + 1 - core}, device_id_type=MESH,
        )

    for which in range(2):
        products(which)
        for p in range(which * per, (which + 1) * per):
            r_copy(p, 0).start()

    for wave in range(pieces + bits):
        for s in reversed(range(1, bits + 1)):
            p = wave + 1 - s
            if 0 <= p < pieces:
                r_finish(p, s - 1)
                if s < bits:
                    r_copy(p, s).start()
                else:
                    f_copy(p).start()
        if wave == 0:
            for off in range(1, members):
                b_arrive(2, off).wait_recv()
            gacc[0] = jnp.sum(gslot[...], axis=0)
        if 0 < wave <= bits:
            g_copy(wave - 1).wait_recv()
            gacc[wave] = gacc[wave - 1] + gland[wave - 1]
        if wave < bits:
            g_copy(wave).start()

    for p in range(pieces):
        which, i = p // per, p % per
        cols = slice(i * pw, (i + 1) * pw)
        mine_rows = pl.ds(pl.multiple_of(home[p] + core * part, 8), part)
        out_ref[2 * which + core, :, cols] = acc[p, mine_rows, :] * scale
    for p in range(pieces):
        which, i = p // per, p % per
        cols = slice(i * pw, (i + 1) * pw)
        f_copy(p).wait_recv()
        out_ref[2 * which + 1 - core, :, cols] = final[p] * scale

    gain_ref[...] = gacc[bits] * scale
    for s in range(bits):
        g_copy(s).wait_send()
    for which in range(3):
        for off in range(1, members):
            b_copy(which, off).wait_send()
    for p in range(pieces):
        for s in range(bits):
            r_copy(p, s).wait_send()
        f_copy(p).wait_send()


def on_device(
    memory, frames, mem_cot, slot_used, key_bias, start_offset, norm_gain, w_query, w_key, w_value, w_out
):
    owners = lax.axis_size("tm")
    groups = lax.axis_size("video")
    position = lax.axis_index("tm")
    streams, rows, features = memory.shape[2:]
    length = frames.shape[3]
    heads = key_bias.shape[3]
    members = 2 * groups
    chips = owners // 2
    bits = chips.bit_length() - 1
    width = features // groups
    keyin = key_rows(frames[0, 0, 0], start_offset[0, 0], position)
    vmem = pl.BlockSpec(memory_space=pltpu.VMEM)
    smem = pl.BlockSpec(memory_space=pltpu.SMEM)
    sds = jax.ShapeDtypeStruct
    pw = 128 if width % 128 == 0 else width
    pieces = 2 * (width // pw)
    dma = pltpu.SemaphoreType.DMA
    grad, weights, gain = pl.pallas_call(
        functools.partial(whole_kernel, owners, groups, heads),
        out_shape=(
            sds((rows, features), F32),
            sds((4, features // owners, width), F32),
            sds((1, features), F32),
        ),
        in_specs=[smem] + [vmem] * 9,
        out_specs=(vmem,) * 3,
        scratch_shapes=[
            pltpu.VMEM((members, length, features), F32),
            pltpu.VMEM((members, rows, features), F32),
            pltpu.VMEM((2, groups, length, width), F32),
            pltpu.VMEM((2, groups, rows, width), F32),
            pltpu.VMEM((1, features), F32),
            pltpu.VMEM((rows, features), F32),
            pltpu.VMEM((2, rows, features), F32),
            pltpu.VMEM((rows, heads * length), F32),
            pltpu.VMEM((rows, heads * length), BF16),
            pltpu.VMEM((heads // 2, 2 * length, 2 * features // heads), BF16),
            pltpu.VMEM((heads // 2, 2 * length, 2 * features // heads), BF16),
            pltpu.VMEM((rows, features), BF16),
            pltpu.VMEM((rows, features), BF16),
            pltpu.VMEM((rows, heads * length), BF16),
            pltpu.VMEM((rows, features), BF16),
            pltpu.VMEM((rows, features), BF16),
            pltpu.VMEM((rows, features), F32),
            pltpu.VMEM((rows, 128), F32),
            pltpu.VMEM((features, features), BF16),
            pltpu.VMEM((features, features), BF16),
            dma((CHUNKS,)), dma((CHUNKS,)), dma((2, members)), dma((2, members)),
            pltpu.VMEM((members, length, width), F32),
            pltpu.VMEM((members, rows, width), F32),
            pltpu.VMEM((features, members * length), BF16),
            pltpu.VMEM((features, members * rows), BF16),
            pltpu.VMEM((pieces, features, pw), F32),
            pltpu.VMEM((pieces, features // owners, pw), F32),
            pltpu.VMEM((members, 1, features), F32),
            pltpu.VMEM((bits + 1, 1, features), F32),
            pltpu.VMEM((max(bits, 1), 1, features), F32),
        ]
        + [pltpu.VMEM((pieces, features >> (s + 1), pw), F32) for s in range(bits)]
        + [
            dma((3, members)), dma((3, members)), dma((pieces, bits)), dma((pieces, bits)),
            dma((bits,)), dma((bits,)), dma((pieces,)), dma((pieces,)),
        ],
        compiler_params=pltpu.CompilerParams(collective_id=0, has_side_effects=True, vmem_limit_bytes=58 * 1024 * 1024),
        name="whole",
    )(
        slot_used[0, 0], memory[0, 0, 0], keyin, mem_cot[0, 0, 0], key_bias[0, 0, 0],
        norm_gain[None, :], w_query, w_key, w_value, w_out,
    )
    return (grad[None, None, None], weights[1], weights[2], weights[3], weights[0], gain[0])


def solution(mesh):
    return jax.shard_map(
        on_device,
        mesh=mesh,
        in_specs=(
            P("video", "tm", None, None, None),
            P("video", "tm", None, None, None),
            P("video", "tm", None, None, None),
            P("video", "tm", None),
            P("video", "tm", None, None, None),
            P("video", None),
            P(),
            P(),
            P(),
            P(),
            P(),
        ),
        out_specs=(
            P("video", "tm", None, None, None),
            P("tm", "video"),
            P("tm", "video"),
            P("tm", "video"),
            P("tm", "video"),
            P(),
        ),
        check_vma=False,
    )
```
